128 devices in a mesh: lat: 8 (over y, z_hi), lon: 16 (over z_lo, x, core).
Axes of the slice: x: 4, y: 4, z: 4 (z_hi: 2, z_lo: 2; z = z_hi * 2 + z_lo), core: 2. Of those that a mesh axis runs over, the one named last changes fastest.
Arguments:
- ocean: float32 [4, 1024, 6144], P(None, ('lat', 'lon')), may hold values from -6 to 6
- grid_mass: float32 [1024, 6144], P('lat', 'lon'), may hold values from 0.5 to 4
- grid_momentum: float32 [2, 1024, 6144], P(None, 'lat', 'lon'), may hold values from -6 to 6
- cells: int32 [4194304], P(('lat', 'lon')), may hold values from 0 to 49151
- offsets: float32 [2, 4194304], P(None, ('lat', 'lon')), may hold values from -0.5 to 0.5
- moves: int32 [4194304], P(('lat', 'lon')), may hold values from 0 to 4, as said below
- slots: int32 [4194304], P(('lat', 'lon')), may hold values from 0 to 8191, as said below
Outputs:
- parcels: float32 [8, 4194304], P(None, ('lat', 'lon'))
- arrivals: float32 [8, 4194304], P(None, ('lat', 'lon'))
The draws below stay inside these ranges and needn't reach their ends.
Inputs may be any that keep to these rules, and one draw needn't show every extreme that they name: `moves`: for each brick and direction the leaving parcels have distinct slots 0 to their count - 1, that count is at most 8192, and in every draw for each direction some brick sends exactly 8192 parcels in it; parcels of the first and last latitude bricks never leave the grid in latitude. `slots`: slots of parcels that stay are 0.
All inputs are finite; a program needn't handle non-finite values.
Results may differ from the reference program's by a relative error of at most 0.0003.
Values sent between devices are 32-bit elements; how exact they have to be, the bound alone decides.
No kernel may reach another device: no remote copies, remote signals or barrier semaphores. Data moves between devices by JAX's collectives and lax.ppermute only.
A program may use at most 128 MiB of HBM per device.

```python
import math
import jax
import jax.numpy as jnp
from jax import lax

GX = 128
GY = 384
P_DEV = 32768
CAP = 8192
NX = 1024
NY = 6144
NPAR = 4194304
N_LAT = 8
N_LON = 16


def migration_plan(key):
    base = jax.random.fold_in(key, 7)
    key_bits, key_pick, key_perm = jax.random.split(base, 3)
    bricks = N_LAT * N_LON
    shift_bits = jax.random.randint(key_bits, (bricks, 4), 0, 3)
    counts = jnp.right_shift(jnp.int32(CAP), shift_bits)
    brick_ids = jnp.arange(bricks, dtype=jnp.int32)
    lat_pos = brick_ids // N_LON
    pick_north = jax.random.randint(jax.random.fold_in(key_pick, 1), (), 0, bricks - N_LON)
    pick_south = jax.random.randint(jax.random.fold_in(key_pick, 2), (), N_LON, bricks)
    pick_east = jax.random.randint(jax.random.fold_in(key_pick, 3), (), 0, bricks)
    pick_west = jax.random.randint(jax.random.fold_in(key_pick, 4), (), 0, bricks)
    picks = jnp.stack([pick_north, pick_south, pick_east, pick_west])
    counts = jnp.where(brick_ids[:, None] == picks[None, :], CAP, counts)
    counts = counts.at[:, 0].set(jnp.where(lat_pos == N_LAT - 1, 0, counts[:, 0]))
    counts = counts.at[:, 1].set(jnp.where(lat_pos == 0, 0, counts[:, 1]))
    ends = jnp.cumsum(counts, axis=1)
    starts = ends - counts
    keys = jax.random.split(key_perm, bricks)
    orders = jax.vmap(lambda each: jax.random.permutation(each, P_DEV))(keys)
    ranks = jnp.argsort(orders, axis=1, stable=True).astype(jnp.int32)
    moves = jnp.zeros((bricks, P_DEV), jnp.int32)
    slots = jnp.zeros((bricks, P_DEV), jnp.int32)
    for direction in range(4):
        inside = (ranks >= starts[:, direction:direction + 1]) & (ranks < ends[:, direction:direction + 1])
        moves = jnp.where(inside, direction + 1, moves)
        slots = jnp.where(inside, ranks - starts[:, direction:direction + 1], slots)
    return (moves.reshape(-1), slots.reshape(-1))


def draw_moves(key, part):
    return migration_plan(key)[0]


def draw_slots(key, part):
    return migration_plan(key)[1]


def set_ends(entries, rng, least, largest):
    dims = entries.shape
    spot = [jax.random.randint(jax.random.fold_in(rng, axis), (), 0, dims[axis]) for axis in range(len(dims))]
    entries = entries.at[tuple(spot)].set(least)
    longest = dims.index(max(dims))
    spot[longest] = (spot[longest] + 1) % dims[longest]
    return entries.at[tuple(spot)].set(largest)


def shard_levels(rng, extent, shards, least, largest):
    factor_of, own = 1.0, jax.random.fold_in(rng, 6)
    for dim, shards_of in shards:
        heights = jnp.exp(jax.random.uniform(jax.random.fold_in(own, dim), (shards_of,), jnp.float32, least / len(shards), largest / len(shards)))
        factor_of = factor_of * jnp.repeat(heights, extent[dim] // shards_of).reshape([-1 if axis == dim else 1 for axis in range(len(extent))])
    return factor_of


def noise(key, extent, deviation, most, pieces=(), kind=jnp.bfloat16):
    loudness = shard_levels(key, extent, pieces, -0.22, 0.18) if pieces else 1.0
    drawn = jax.random.normal(key, extent, jnp.float32) * deviation * loudness
    return jnp.minimum(jnp.maximum(drawn, -most), most).astype(kind)


def setup_inputs(seed: int = 0) -> dict:
    arg_keys = jax.random.split(jax.random.key(seed), 8)
    return {
        "ocean": noise(arg_keys[0], (4, NX, NY), 1.0, 6.0, ((1, 128),), jnp.float32),
        "grid_mass": jnp.clip(jnp.exp(math.log(4.0) - 2.0794415 * jax.random.uniform(arg_keys[1], (NX, NY), jnp.float32) ** shard_levels(arg_keys[1], (NX, NY), ((0, 8), (1, 16)), -0.2, 0.2)), 0.5, 4.0),
        "grid_momentum": noise(arg_keys[2], (2, NX, NY), 1.0, 6.0, ((1, 8), (2, 16)), jnp.float32),
        "cells": set_ends(jax.random.randint(arg_keys[3], (NPAR,), 0, GX * GY), jax.random.fold_in(arg_keys[3], 1), 0, (GX * GY) - 1).astype(jnp.int32),
        "offsets": jnp.clip(jax.random.uniform(arg_keys[4], (2, NPAR), jnp.float32, -0.5, 0.5) * shard_levels(arg_keys[4], (2, NPAR), ((1, 128),), -0.4, 0.0), -0.5, 0.5),
        "moves": draw_moves(jax.random.fold_in(arg_keys[7], 71), 0),
        "slots": draw_slots(jax.random.fold_in(arg_keys[7], 71), 0),
    }


step_dt = 0.5
drag_coef = 2.0


def spline(frac):
    lower = 0.5 * (0.5 - frac) * (0.5 - frac)
    middle = 0.75 - frac * frac
    upper = 0.5 * (0.5 + frac) * (0.5 + frac)
    return (lower, middle, upper)


def interpolate(fetch, frac):
    weights_row = spline(frac[0])
    weights_col = spline(frac[1])
    speed = jnp.zeros(frac.shape, jnp.float32)
    affine = jnp.zeros((4, frac.shape[1]), jnp.float32)
    for row_step in (-1, 0, 1):
        for col_step in (-1, 0, 1):
            weight = weights_row[row_step + 1] * weights_col[col_step + 1]
            sample = fetch(row_step, col_step)
            speed = speed + weight * sample
            arm_row = row_step - frac[0]
            arm_col = col_step - frac[1]
            terms = jnp.stack([sample[0] * arm_row, sample[0] * arm_col, sample[1] * arm_row, sample[1] * arm_col])
            affine = affine + 4.0 * weight * terms
    return jnp.concatenate([frac + step_dt * speed, speed, affine], axis=0)


def reference(ocean, grid_mass, grid_momentum, cells, offsets, moves, slots):
    current = ocean[0:2]
    stress = ocean[2:4]
    velocity = (grid_momentum + step_dt * stress + step_dt * drag_coef * grid_mass * current) / (grid_mass * (1.0 + step_dt * drag_coef))
    padded = jnp.pad(velocity, ((0, 0), (1, 1), (0, 0)))
    bricks = N_LAT * N_LON
    total_slots = 4 * CAP * bricks
    frac_all = offsets.reshape(2, bricks, P_DEV).transpose(1, 0, 2)
    cell_all = cells.reshape(bricks, P_DEV)
    move_all = moves.reshape(bricks, P_DEV)
    slot_all = slots.reshape(bricks, P_DEV)
    brick_ids = jnp.arange(bricks, dtype=jnp.int32)

    def one_brick(arrived, inputs):
        brick, cell, frac, move, slot = inputs
        lat_pos = brick // N_LON
        lon_pos = brick % N_LON
        row = lat_pos * GX + cell // GY + 1
        column = lon_pos * GY + cell % GY

        def fetch(row_step, col_step):
            return padded[:, row + row_step, (column + col_step) % NY]

        state = interpolate(fetch, frac)
        dest_lat = jnp.where(move == 1, lat_pos + 1, jnp.where(move == 2, lat_pos - 1, lat_pos))
        dest_lon = jnp.where(move == 3, (lon_pos + 1) % N_LON, jnp.where(move == 4, (lon_pos + N_LON - 1) % N_LON, lon_pos))
        target = (dest_lat * N_LON + dest_lon) * (4 * CAP) + (move - 1) * CAP + slot
        target = jnp.where(move > 0, target, total_slots).astype(jnp.int32)
        arrived = arrived.at[:, target].set(state, mode="drop")
        return arrived, state

    start = jnp.zeros((8, total_slots), jnp.float32)
    arrivals, states = lax.scan(one_brick, start, (brick_ids, cell_all, frac_all, move_all, slot_all))
    parcels = states.transpose(1, 0, 2).reshape(8, bricks * P_DEV)
    return parcels, arrivals
```

```python
import jax
import jax.numpy as jnp
from jax import lax
from jax.experimental import pallas as pl
from jax.experimental.pallas import tpu as pltpu
from jax.sharding import PartitionSpec as P

CAP = 8192
ROWS = 128
COLS = 384
BLOCKS = 3
VREGS = 32
PAD_ROWS = 144
PLANE = BLOCKS * PAD_ROWS

step_dt = 0.5
drag_coef = 2.0

f32 = jnp.float32
i32 = jnp.int32


def lane_ids():
    return lax.broadcasted_iota(i32, (8, 128), 1)


def sublane_ids():
    return lax.broadcasted_iota(i32, (8, 128), 0)


def from_lanes(x, index):
    return jnp.take_along_axis(x, index, axis=1, mode="promise_in_bounds")


def from_sublanes(x, index):
    return jnp.take_along_axis(x, index, axis=0, mode="promise_in_bounds")


def bit_set(words, place):
    return lax.shift_left(words, 31 - place) < 0


def lane_pass(xs, distance_bit, flips):
    lane = lane_ids()
    perm = lane ^ lax.shift_left(1, distance_bit)
    place = lax.shift_right_logical(lane, distance_bit) & 1
    uppers = [(place ^ flip) != 0 for flip in flips]
    out = []
    for v, x in enumerate(xs):
        other = from_lanes(x, perm)
        out.append(
            jnp.where(uppers[v % len(uppers)], jnp.maximum(x, other), jnp.minimum(x, other))
        )
    return tuple(out)


def sort_network(key, payloads, index_out, word_out, sub_word_out):
    lane = lane_ids()
    sub = sublane_ids()

    xs = tuple((key[v] & -128) | lane for v in range(VREGS))

    def early_stage(k, xs):
        flip = lax.shift_right_logical(lane, k) & 1

        def one(step, xs):
            return lane_pass(xs, k - 1 - step, (flip,))

        return lax.fori_loop(0, k, one, xs)

    xs = lax.fori_loop(1, 7, early_stage, xs)
    xs = lax.fori_loop(0, 7, lambda step, xs: lane_pass(xs, 6 - step, (0, 1)), xs)
    for v in range(VREGS):
        key[v] = xs[v]
        index = xs[v] & 127
        if index_out is not None:
            index_out[0, v] = index
            word_out[v] = jnp.zeros((8, 128), i32)
            sub_word_out[v] = jnp.zeros((8, 128), i32)
        for payload in payloads:
            payload[v] = from_lanes(payload[v], index)

    def stage(t, carry):
        def flip_of(v):
            return -(lax.shift_right_logical(sub * 32 + v, t) & 1)

        for v in range(VREGS):
            key[v] = key[v] ^ flip_of(v)

        for i in (7, 6, 5):

            @pl.when(i < t)
            def _():
                near = i - 5
                perm = sub ^ (1 << near)
                upper = (lax.shift_right_logical(sub, near) & 1) != 0
                place = jnp.where(t == 6, 0, jnp.where(t == 7, 1, 3)) + t - 1 - i
                for v in range(VREGS):
                    x = key[v]
                    other = from_sublanes(x, perm)
                    take = jnp.where(upper, other, x) > jnp.where(upper, x, other)
                    key[v] = jnp.where(take, other, x)
                    if index_out is not None:
                        sub_word_out[v] = sub_word_out[v] | jnp.where(
                            take, lax.shift_left(1, place), 0
                        )
                    for payload in payloads:
                        y = payload[v]
                        payload[v] = jnp.where(take, from_sublanes(y, perm), y)

        for i in (4, 3, 2, 1, 0):

            @pl.when(i < t)
            def _():
                place = jnp.where(t <= 5, t * (t - 1) // 2, 5 * t - 15) + t - 1 - i
                place = jnp.where(t <= 5, place, 5 * t - 15 + 4 - i)
                for a in range(VREGS):
                    if a & (1 << i):
                        continue
                    b = a | (1 << i)
                    x, y = key[a], key[b]
                    swap = x > y
                    key[a] = jnp.minimum(x, y)
                    key[b] = jnp.maximum(x, y)
                    if index_out is not None:
                        word_out[a] = word_out[a] | jnp.where(swap, lax.shift_left(1, place), 0)
                    for payload in payloads:
                        x, y = payload[a], payload[b]
                        payload[a] = jnp.where(swap, y, x)
                        payload[b] = jnp.where(swap, x, y)

        xs = []
        for v in range(VREGS):
            flip = flip_of(v)
            xs.append((((key[v] ^ flip) & -128) | lane) ^ flip)
        xs = lax.fori_loop(0, 7, lambda step, xs: lane_pass(xs, 6 - step, (0,)), tuple(xs))
        for v in range(VREGS):
            x = xs[v] ^ flip_of(v)
            key[v] = x
            index = x & 127
            if index_out is not None:
                index_out[t, v] = index
            for payload in payloads:
                payload[v] = from_lanes(payload[v], index)
        return carry

    lax.fori_loop(1, 9, stage, 0)


def row_place(t, i):
    return t * (t - 1) // 2 + t - 1 - i if t <= 5 else 5 * t - 15 + 4 - i


def sub_place(t, i):
    return {6: 0, 7: 1, 8: 3}[t] + t - 1 - i


def apply_network(xs, index, words, sub_words):
    sub = sublane_ids()
    xs = [from_lanes(xs[v], index[0, v]) for v in range(VREGS)]
    for t in range(1, 9):
        for i in range(t - 1, -1, -1):
            if i >= 5:
                perm = sub ^ (1 << (i - 5))
                place = sub_place(t, i)
                xs = [
                    jnp.where(bit_set(sub_words[v], place), from_sublanes(xs[v], perm), xs[v])
                    for v in range(VREGS)
                ]
            else:
                place = row_place(t, i)
                for a in range(VREGS):
                    if a & (1 << i):
                        continue
                    b = a | (1 << i)
                    swap = bit_set(words[a], place)
                    x, y = xs[a], xs[b]
                    xs[a] = jnp.where(swap, y, x)
                    xs[b] = jnp.where(swap, x, y)
        xs = [from_lanes(xs[v], index[t, v]) for v in range(VREGS)]
    return xs


def plan_kernel(
    cells, offsets, moves, slots,
    near_out, frac_out, counts_out,
    index_a, word_a, sub_a, index_b, word_b, sub_b,
    key, tags,
):
    lane = lane_ids()
    sub = sublane_ids()
    stay = jnp.where(moves[...] == 0, 1.0, 0.0)
    before = jnp.where(
        lax.broadcasted_iota(i32, (128, 128), 0) < lax.broadcasted_iota(i32, (128, 128), 1), 1.0, 0.0
    )
    rank = jnp.dot(stay, before, preferred_element_type=f32)
    above = jnp.where(
        lax.broadcasted_iota(i32, (256, 256), 1) < lax.broadcasted_iota(i32, (256, 256), 0), 1.0, 0.0
    )
    totals = jnp.broadcast_to(jnp.sum(stay, axis=1, keepdims=True), (256, 128))
    rank = rank + jnp.dot(above, totals, preferred_element_type=f32)
    rank = rank.astype(i32)
    counts = []
    for k in range(4):
        count = jnp.sum(jnp.where(moves[...] == k + 1, 1.0, 0.0)).astype(i32)
        counts.append(count)
        counts_out[k] = count
    hole = rank + counts[0]
    filled = counts[0]
    for k in range(1, 4):
        hole = hole + jnp.where(rank >= k * CAP - filled, counts[k], 0)
        filled = filled + counts[k]
    target = jnp.where(moves[...] > 0, (moves[...] - 1) * CAP + slots[...], hole)
    number = lax.broadcasted_iota(i32, (256, 128), 0) * 128 + lax.broadcasted_iota(i32, (256, 128), 1)
    cell = cells[...]
    row = (cell.astype(f32) * (1.0 / COLS)).astype(i32)
    row = row - jnp.where(row * COLS > cell, 1, 0)
    row = row + jnp.where((row + 1) * COLS <= cell, 1, 0)
    col = cell - row * COLS
    spot = lax.shift_right_logical(col, 7) * (ROWS * 128) + row * 128 + (col & 127)
    for v in range(VREGS):
        part = slice(v * 8, v * 8 + 8)
        key[v] = lax.shift_left(spot[part], 7)
        tags[v] = lax.shift_left(target[part], 15) | number[part]
        frac_out[0, v] = offsets[0, part]
        frac_out[1, v] = offsets[1, part]
    sort_network(key, (frac_out.at[0], frac_out.at[1], tags), None, None, None)
    for v in range(VREGS):
        near_out[v] = lax.shift_right_logical(key[v], 7)
        key[v] = lax.shift_left(lax.shift_right_logical(tags[v], 15), 7)
    sort_network(key, (), index_a, word_a, sub_a)
    for v in range(VREGS):
        key[v] = lax.shift_left(tags[v] & 32767, 7)
    sort_network(key, (), index_b, word_b, sub_b)


def plan(cells, offsets, moves, slots):
    vmem = pl.BlockSpec(memory_space=pltpu.VMEM)
    smem = pl.BlockSpec(memory_space=pltpu.SMEM)
    network = [
        jax.ShapeDtypeStruct((9, VREGS, 8, 128), i32),
        jax.ShapeDtypeStruct((VREGS, 8, 128), i32),
        jax.ShapeDtypeStruct((VREGS, 8, 128), i32),
    ]
    return pl.pallas_call(
        plan_kernel,
        out_shape=[
            jax.ShapeDtypeStruct((VREGS, 8, 128), i32),
            jax.ShapeDtypeStruct((2, VREGS, 8, 128), f32),
            jax.ShapeDtypeStruct((4,), i32),
        ]
        + network
        + network,
        in_specs=[vmem] * 4,
        out_specs=[vmem, vmem, smem] + [vmem] * 6,
        scratch_shapes=[pltpu.VMEM((VREGS, 8, 128), i32), pltpu.VMEM((VREGS, 8, 128), i32)],
        compiler_params=pltpu.CompilerParams(vmem_limit_bytes=32 << 20),
        cost_estimate=pl.CostEstimate(flops=20_000_000, bytes_accessed=8_000_000, transcendentals=0),
        name="plan",
    )(cells.reshape(256, 128), offsets.reshape(2, 256, 128), moves.reshape(256, 128), slots.reshape(256, 128))


def velocity_kernel(forcing, mass, momentum, out):
    heavy = mass[...]
    for part in range(2):
        current = forcing[:, part].reshape(ROWS, COLS)
        stress = forcing[:, 2 + part].reshape(ROWS, COLS)
        out[part] = (momentum[part] + step_dt * stress + step_dt * drag_coef * heavy * current) / (
            heavy * (1.0 + step_dt * drag_coef)
        )


def node_velocity(forcing, mass, momentum):
    vmem = pl.BlockSpec(memory_space=pltpu.VMEM)
    return pl.pallas_call(
        velocity_kernel,
        out_shape=jax.ShapeDtypeStruct((2, ROWS, COLS), f32),
        in_specs=[vmem] * 3,
        out_specs=vmem,
        name="velocity",
    )(forcing, mass, momentum)


def table_kernel(velocity, west, east, table, first_edge, last_edge):
    lane = lax.broadcasted_iota(i32, (ROWS, 128), 1)
    for part in range(2):
        blocks = [velocity[part, :, 128 * k : 128 * k + 128] for k in range(BLOCKS)]
        left = [west[part]] + blocks[:-1]
        right = blocks[1:] + [east[part]]
        for k in range(BLOCKS):
            shifted = [
                jnp.where(lane == 0, pltpu.roll(left[k], 1, 1), pltpu.roll(blocks[k], 1, 1)),
                blocks[k],
                jnp.where(lane == 127, pltpu.roll(right[k], 127, 1), pltpu.roll(blocks[k], 127, 1)),
            ]
            for q in range(3):
                plane = part * 3 + q
                table[plane, k] = shifted[q]
                first_edge[plane, k] = shifted[q][0:1]
                last_edge[plane, k] = shifted[q][ROWS - 1 : ROWS]


def node_table(velocity, west, east):
    vmem = pl.BlockSpec(memory_space=pltpu.VMEM)
    return pl.pallas_call(
        table_kernel,
        out_shape=[
            jax.ShapeDtypeStruct((6, BLOCKS, ROWS, 128), f32),
            jax.ShapeDtypeStruct((6, BLOCKS, 1, 128), f32),
            jax.ShapeDtypeStruct((6, BLOCKS, 1, 128), f32),
        ],
        in_specs=[vmem] * 3,
        out_specs=[vmem] * 3,
        name="table",
    )(velocity, west, east)


def spline(frac):
    lower = 0.5 * (0.5 - frac) * (0.5 - frac)
    middle = 0.75 - frac * frac
    upper = 0.5 * (0.5 + frac) * (0.5 + frac)
    return (lower, middle, upper)


def transfer_kernel(
    first, last, spans, counts,
    table, above, below, near, frac, index, words, sub_words,
    state, north, south, east, west,
    nodes, samples, columns,
):
    nodes[6 * PLANE : 8 * PLANE, :] = jnp.zeros((2 * PLANE, 128), f32)
    for plane in range(6):
        for k in range(BLOCKS):
            base = plane * PLANE + k * PAD_ROWS
            nodes[base + 8 : base + 8 + ROWS, :] = table[plane, k]
            nodes[base + 7 : base + 8, :] = above[plane, k]
            nodes[base + 8 + ROWS : base + 9 + ROWS, :] = below[plane, k]

    def group(v, carry):
        def chunk(step, sums):
            sums = list(sums)
            for s in range(8):
                block = v * 8 + s
                here = jnp.minimum(first[block] + step, last[block])
                base = here + lax.shift_right_logical(here, 7) * 16 + 8
                spot = near[pl.ds(block, 8, stride=0), :]
                lanes = spot & 127
                inside = lax.shift_right_logical(spot, 7) == here
                for r in range(3):
                    got = from_lanes(nodes[pl.ds(base + r - 1, 8, stride=PLANE), :], lanes)
                    sums[3 * s + r] = jnp.where(inside, got, sums[3 * s + r])
            return tuple(sums)

        sums = lax.fori_loop(0, spans[v], chunk, tuple(jnp.zeros((8, 128), f32) for _ in range(24)))
        for s in range(8):
            for r in range(3):
                samples[pl.ds(r * 2048 + v * 8 + s, 8, stride=256), :] = sums[3 * s + r]
        here = pl.ds(pl.multiple_of(v * 8, 8), 8)
        d_row = frac[0, v]
        d_col = frac[1, v]
        w_row = spline(d_row)
        w_col = spline(d_col)
        arm_row = [4.0 * w_row[r] * (r - 1 - d_row) for r in range(3)]
        arm_col = [4.0 * w_col[q] * (q - 1 - d_col) for q in range(3)]
        speeds = []
        affines = []
        for part in range(2):
            speed = along_row = along_col = None
            for q in range(3):
                plane = part * 3 + q
                got = [
                    samples[pl.ds(pl.multiple_of(r * 2048 + plane * 256 + v * 8, 8), 8), :]
                    for r in range(3)
                ]
                plain = w_row[0] * got[0] + w_row[1] * got[1] + w_row[2] * got[2]
                tilted = arm_row[0] * got[0] + arm_row[1] * got[1] + arm_row[2] * got[2]
                terms = (w_col[q] * plain, w_col[q] * tilted, arm_col[q] * plain)
                if q == 0:
                    speed, along_row, along_col = terms
                else:
                    speed = speed + terms[0]
                    along_row = along_row + terms[1]
                    along_col = along_col + terms[2]
            speeds.append(speed)
            affines += [along_row, along_col]
        values = [d_row + step_dt * speeds[0], d_col + step_dt * speeds[1]] + speeds + affines
        for c in range(8):
            state[c, v] = values[c]
        return carry

    lax.fori_loop(0, VREGS, group, 0)

    lane = lane_ids()
    sub = sublane_ids()

    def component(c, carry):
        xs = apply_network([state[c, v] for v in range(VREGS)], index, words, sub_words)
        direction = lax.shift_right_logical(sub, 1)
        count = jnp.where(
            direction < 2,
            jnp.where(direction == 0, counts[0], counts[1]),
            jnp.where(direction == 2, counts[2], counts[3]),
        )
        slot = (sub & 1) * 4096 + lane
        for v in range(VREGS):
            kept = jnp.where(slot + v * 128 < count, xs[v], 0.0)
            columns[pl.ds(v * 8 + c, 8, stride=256), :] = kept
        return carry

    lax.fori_loop(0, 8, component, 0)
    for k, out in enumerate((north, south, east, west)):
        for j in range(64):
            base = (k * 64 + j) * 8
            out[:, 128 * j : 128 * j + 128] = columns[base : base + 8, :]


def transfer(bounds, spans, counts, table, above, below, near, frac, network):
    vmem = pl.BlockSpec(memory_space=pltpu.VMEM)
    smem = pl.BlockSpec(memory_space=pltpu.SMEM)
    return pl.pallas_call(
        transfer_kernel,
        out_shape=[jax.ShapeDtypeStruct((8, VREGS, 8, 128), f32)]
        + [jax.ShapeDtypeStruct((8, CAP), f32)] * 4,
        in_specs=[smem] * 4 + [vmem] * 8,
        out_specs=[vmem] * 5,
        scratch_shapes=[
            pltpu.VMEM((8 * PLANE, 128), f32),
            pltpu.VMEM((3 * 2048, 128), f32),
            pltpu.VMEM((2048, 128), f32),
        ],
        compiler_params=pltpu.CompilerParams(vmem_limit_bytes=40 << 20),
        cost_estimate=pl.CostEstimate(flops=20_000_000, bytes_accessed=8_000_000, transcendentals=0),
        name="transfer",
    )(bounds[0], bounds[1], spans, counts, table, above, below, near.reshape(256, 128), frac, *network)


def restore_kernel(state, index, words, sub_words, out, columns):
    def component(c, carry):
        xs = apply_network([state[c, v] for v in range(VREGS)], index, words, sub_words)
        for v in range(VREGS):
            columns[pl.ds(v * 8 + c, 8, stride=256), :] = xs[v]
        return carry

    lax.fori_loop(0, 8, component, 0)
    for j in range(256):
        out[:, 128 * j : 128 * j + 128] = columns[8 * j : 8 * j + 8, :]


def restore(state, network):
    vmem = pl.BlockSpec(memory_space=pltpu.VMEM)
    return pl.pallas_call(
        restore_kernel,
        out_shape=jax.ShapeDtypeStruct((8, 4 * CAP), f32),
        in_specs=[vmem] * 4,
        out_specs=vmem,
        scratch_shapes=[pltpu.VMEM((2048, 128), f32)],
        compiler_params=pltpu.CompilerParams(vmem_limit_bytes=32 << 20),
        cost_estimate=pl.CostEstimate(flops=10_000_000, bytes_accessed=4_000_000, transcendentals=0),
        name="restore",
    )(state, *network)


def from_behind(block, axis, distance):
    devices = range(lax.axis_size(axis))
    route = [(i - distance, i) for i in devices if i - distance in devices]
    return lax.ppermute(block, axis, route)


def passed_along(value, axis, by):
    count = lax.axis_size(axis)
    return lax.ppermute(value, axis, [(i, (i + by) % count) for i in range(count)])


def shards(ocean, grid_mass, grid_momentum, cells, offsets, moves, slots):
    outgoing = ocean.reshape(4, 8, 16, COLS).transpose(2, 0, 1, 3)
    forcing = lax.all_to_all(outgoing, "lon", 0, 0)
    planned = plan(cells, offsets, moves, slots)
    near, frac, counts = planned[:3]
    slot_network, home_network = planned[3:6], planned[6:9]
    ends = lax.shift_right_logical(near.reshape(256, 128), 7)
    bounds = (ends[:, 0], ends[:, 127])
    spans = jnp.max((bounds[1] - bounds[0]).reshape(VREGS, 8), axis=1) + 1
    velocity = node_velocity(forcing, grid_mass, grid_momentum)
    west = passed_along(velocity[:, :, COLS - 128 :], "lon", 1)
    east = passed_along(velocity[:, :, :128], "lon", -1)
    table, first_edge, last_edge = node_table(velocity, west, east)
    above = from_behind(last_edge, "lat", 1)
    below = from_behind(first_edge, "lat", -1)
    state, north, south, east, west = transfer(
        bounds, spans, counts, table, above, below, near, frac, slot_network
    )
    north = from_behind(north, "lat", 1)
    south = from_behind(south, "lat", -1)
    east = passed_along(east, "lon", 1)
    west = passed_along(west, "lon", -1)
    parcels = restore(state, home_network)
    return (parcels, jnp.concatenate([north, south, east, west], axis=1))


def solution(mesh):
    in_specs = (
        P(None, ("lat", "lon"), None),
        P("lat", "lon"),
        P(None, "lat", "lon"),
        P(("lat", "lon")),
        P(None, ("lat", "lon")),
        P(("lat", "lon")),
        P(("lat", "lon")),
    )
    out_specs = (P(None, ("lat", "lon")), P(None, ("lat", "lon")))
    return jax.shard_map(shards, mesh=mesh, in_specs=in_specs, out_specs=out_specs, check_vma=False)
```

```python
import jax
import jax.numpy as jnp
from jax import lax
from jax.experimental import pallas as pl
from jax.experimental.pallas import tpu as pltpu
from jax.sharding import PartitionSpec as P

CAP = 8192
ROWS = 128
COLS = 384
BLOCKS = 3
VREGS = 32
PAD_ROWS = 144
PLANE = BLOCKS * PAD_ROWS

step_dt = 0.5
drag_coef = 2.0

f32 = jnp.float32
i32 = jnp.int32


def lane_ids():
    return lax.broadcasted_iota(i32, (8, 128), 1)


def sublane_ids():
    return lax.broadcasted_iota(i32, (8, 128), 0)


def from_lanes(x, index):
    return jnp.take_along_axis(x, index, axis=1, mode="promise_in_bounds")


def from_sublanes(x, index):
    return jnp.take_along_axis(x, index, axis=0, mode="promise_in_bounds")


def bit_set(words, place):
    return lax.shift_left(words, 31 - place) < 0


def lane_pass(xs, distance_bit, uppers, perm):
    out = []
    for v, x in enumerate(xs):
        other = from_lanes(x, perm)
        out.append(
            jnp.where(uppers[v % len(uppers)], jnp.maximum(x, other), jnp.minimum(x, other))
        )
    return out


def lane_bit(k):
    return lax.shift_right_logical(lane_ids(), k) & 1


def lane_passes(xs, top, flips):
    lane = lane_ids()
    for j in range(top, -1, -1):
        uppers = [(lane_bit(j) ^ flip) != 0 for flip in flips]
        xs = lane_pass(xs, j, uppers, lane ^ (1 << j))
    return xs


def sort_network(keys, payloads, record):
    lane = lane_ids()
    lane_f = lane.astype(f32)
    sub = sublane_ids()
    words = [jnp.zeros((8, 128), i32) for _ in range(VREGS)] if record else None
    sub_words = [jnp.zeros((8, 128), i32) for _ in range(VREGS)] if record else None

    xs = [key * 128.0 + lane_f for key in keys]
    for k in range(1, 7):
        xs = lane_passes(xs, k - 1, (lane_bit(k),))
    xs = lane_passes(xs, 6, (0, 1))

    def settle(t, xs):
        out = []
        for v in range(VREGS):
            index = xs[v].astype(i32) & 127
            if record:
                record(t, v, index)
            for payload in payloads:
                payload[v] = from_lanes(payload[v], index)
            out.append(xs[v] - index.astype(f32) + lane_f)
        return out

    xs = settle(0, xs)
    for t in range(1, 9):
        sign = None
        if 5 <= t <= 7:
            sign = jnp.where((lax.shift_right_logical(sub, t - 5) & 1) != 0, -1.0, 1.0)
            xs = [x * sign for x in xs]
        for i in range(t - 1, -1, -1):
            if i >= 5:
                near = i - 5
                perm = sub ^ (1 << near)
                upper = (lax.shift_right_logical(sub, near) & 1) != 0
                for v in range(VREGS):
                    x = xs[v]
                    other = from_sublanes(x, perm)
                    take = jnp.where(upper, other, x) > jnp.where(upper, x, other)
                    xs[v] = jnp.where(take, other, x)
                    if record:
                        sub_words[v] = sub_words[v] | jnp.where(take, 1 << sub_place(t, i), 0)
                    for payload in payloads:
                        y = payload[v]
                        payload[v] = jnp.where(take, from_sublanes(y, perm), y)
            else:
                for a in range(VREGS):
                    if a & (1 << i):
                        continue
                    b = a | (1 << i)
                    x, y = xs[a], xs[b]
                    down = t <= 4 and (a >> t) & 1
                    swap = x < y if down else x > y
                    low, high = jnp.minimum(x, y), jnp.maximum(x, y)
                    xs[a], xs[b] = (high, low) if down else (low, high)
                    if record:
                        words[a] = words[a] | jnp.where(swap, 1 << row_place(t, i), 0)
                    for payload in payloads:
                        x, y = payload[a], payload[b]
                        payload[a] = jnp.where(swap, y, x)
                        payload[b] = jnp.where(swap, x, y)
        if t <= 4:
            runs = [xs[v] for v in range(VREGS)]
            lane_done = []
            ups = [v for v in range(VREGS) if not (v >> t) & 1]
            downs = [v for v in range(VREGS) if (v >> t) & 1]
            up_x = lane_passes([runs[v] for v in ups], 6, (0,))
            down_x = lane_passes([runs[v] for v in downs], 6, (1,)) if downs else []
            for v, x in zip(ups, up_x):
                xs[v] = x
            for v, x in zip(downs, down_x):
                xs[v] = x
        else:
            xs = lane_passes(xs, 6, (0,))
            if sign is not None:
                xs = [x * sign for x in xs]
        xs = settle(t, xs)
    return xs, words, sub_words


def row_place(t, i):
    return t * (t - 1) // 2 + t - 1 - i if t <= 5 else 5 * t - 15 + 4 - i


def sub_place(t, i):
    return {6: 0, 7: 1, 8: 3}[t] + t - 1 - i


def apply_network(count, source, buffer, index, words, sub_words, finish):
    sub = sublane_ids()
    for v in range(VREGS):
        lanes = index[0, v]
        for c in range(count):
            buffer[c, v] = from_lanes(source(c, v), lanes)
    for t in range(1, 9):
        steps = [i for i in range(t - 1, -1, -1) if i >= 5]
        if steps:
            for v in range(VREGS):
                takes = [bit_set(sub_words[v], sub_place(t, i)) for i in steps]
                for c in range(count):
                    x = buffer[c, v]
                    for i, take in zip(steps, takes):
                        x = jnp.where(take, from_sublanes(x, sub ^ (1 << (i - 5))), x)
                    buffer[c, v] = x
        top = min(t, 5)
        rounds = {1: ((0,),), 2: ((1, 0),), 3: ((2, 1, 0),), 4: ((3, 2), (1, 0)), 5: ((4, 3), (2, 1, 0))}[top]
        for bits in rounds:
            mask = sum(1 << i for i in bits)
            for base in range(VREGS):
                if base & mask:
                    continue
                members = [v for v in range(VREGS) if v & ~mask == base]
                swaps = {}
                for i in bits:
                    for a in members:
                        if not a & (1 << i):
                            swaps[i, a] = bit_set(words[a], row_place(t, i))
                for c in range(count):
                    xs = {v: buffer[c, v] for v in members}
                    for i in bits:
                        for a in members:
                            if a & (1 << i):
                                continue
                            b = a | (1 << i)
                            x, y = xs[a], xs[b]
                            xs[a] = jnp.where(swaps[i, a], y, x)
                            xs[b] = jnp.where(swaps[i, a], x, y)
                    for v in members:
                        buffer[c, v] = xs[v]
        for v in range(VREGS):
            lanes = index[t, v]
            moved = [from_lanes(buffer[c, v], lanes) for c in range(count)]
            if t < 8:
                for c in range(count):
                    buffer[c, v] = moved[c]
            else:
                finish(v, moved)


def plan_kernel(
    cells, offsets, moves, slots,
    near_out, frac_out, counts_out,
    index_out, words_out,
    tags,
):
    lane = lane_ids()
    sub = sublane_ids()
    stay = jnp.where(moves[...] == 0, 1.0, 0.0)
    before = jnp.where(
        lax.broadcasted_iota(i32, (128, 128), 0) < lax.broadcasted_iota(i32, (128, 128), 1), 1.0, 0.0
    )
    rank = jnp.dot(stay, before, preferred_element_type=f32)
    above = jnp.where(
        lax.broadcasted_iota(i32, (256, 256), 1) < lax.broadcasted_iota(i32, (256, 256), 0), 1.0, 0.0
    )
    totals = jnp.broadcast_to(jnp.sum(stay, axis=1, keepdims=True), (256, 128))
    rank = rank + jnp.dot(above, totals, preferred_element_type=f32)
    rank = rank.astype(i32)
    counts = []
    for k in range(4):
        count = jnp.sum(jnp.where(moves[...] == k + 1, 1.0, 0.0)).astype(i32)
        counts.append(count)
        counts_out[k] = count
    hole = rank + counts[0]
    filled = counts[0]
    for k in range(1, 4):
        hole = hole + jnp.where(rank >= k * CAP - filled, counts[k], 0)
        filled = filled + counts[k]
    target = jnp.where(moves[...] > 0, (moves[...] - 1) * CAP + slots[...], hole)
    number = lax.broadcasted_iota(i32, (256, 128), 0) * 128 + lax.broadcasted_iota(i32, (256, 128), 1)
    cell = cells[...]
    row = (cell.astype(f32) * (1.0 / COLS)).astype(i32)
    row = row - jnp.where(row * COLS > cell, 1, 0)
    row = row + jnp.where((row + 1) * COLS <= cell, 1, 0)
    col = cell - row * COLS
    spot = lax.shift_right_logical(col, 7) * (ROWS * 128) + row * 128 + (col & 127)
    keys = []
    for v in range(VREGS):
        part = slice(v * 8, v * 8 + 8)
        keys.append(spot[part].astype(f32))
        tags[v] = lax.shift_left(target[part], 15) | number[part]
        frac_out[0, v] = offsets[0, part]
        frac_out[1, v] = offsets[1, part]
    keys, _, _ = sort_network(keys, (frac_out.at[0], frac_out.at[1], tags), None)
    for v in range(VREGS):
        near_out[v] = lax.shift_right_logical(keys[v].astype(i32), 7)

    def one(which, carry):
        keys = [
            (lax.shift_right_logical(tags[v], jnp.where(which == 0, 15, 0)) & 32767).astype(f32)
            for v in range(VREGS)
        ]

        def record(t, v, index):
            index_out[which, t, v] = index

        _, words, sub_words = sort_network(keys, (), record)
        for v in range(VREGS):
            words_out[which, 0, v] = words[v]
            words_out[which, 1, v] = sub_words[v]
        return carry

    lax.fori_loop(0, 2, one, 0)


def plan(cells, offsets, moves, slots):
    vmem = pl.BlockSpec(memory_space=pltpu.VMEM)
    smem = pl.BlockSpec(memory_space=pltpu.SMEM)
    return pl.pallas_call(
        plan_kernel,
        out_shape=[
            jax.ShapeDtypeStruct((VREGS, 8, 128), i32),
            jax.ShapeDtypeStruct((2, VREGS, 8, 128), f32),
            jax.ShapeDtypeStruct((4,), i32),
            jax.ShapeDtypeStruct((2, 9, VREGS, 8, 128), i32),
            jax.ShapeDtypeStruct((2, 2, VREGS, 8, 128), i32),
        ],
        in_specs=[vmem] * 4,
        out_specs=[vmem, vmem, smem, vmem, vmem],
        scratch_shapes=[pltpu.VMEM((VREGS, 8, 128), i32)],
        compiler_params=pltpu.CompilerParams(vmem_limit_bytes=32 << 20),
        cost_estimate=pl.CostEstimate(flops=20_000_000, bytes_accessed=8_000_000, transcendentals=0),
        name="plan",
    )(cells.reshape(256, 128), offsets.reshape(2, 256, 128), moves.reshape(256, 128), slots.reshape(256, 128))


def velocity_kernel(forcing, mass, momentum, out):
    heavy = mass[...]
    for part in range(2):
        current = forcing[:, part].reshape(ROWS, COLS)
        stress = forcing[:, 2 + part].reshape(ROWS, COLS)
        out[part] = (momentum[part] + step_dt * stress + step_dt * drag_coef * heavy * current) / (
            heavy * (1.0 + step_dt * drag_coef)
        )


def node_velocity(forcing, mass, momentum):
    vmem = pl.BlockSpec(memory_space=pltpu.VMEM)
    return pl.pallas_call(
        velocity_kernel,
        out_shape=jax.ShapeDtypeStruct((2, ROWS, COLS), f32),
        in_specs=[vmem] * 3,
        out_specs=vmem,
        name="velocity",
    )(forcing, mass, momentum)


def table_kernel(velocity, west, east, table, first_edge, last_edge):
    lane = lax.broadcasted_iota(i32, (ROWS, 128), 1)
    for part in range(2):
        blocks = [velocity[part, :, 128 * k : 128 * k + 128] for k in range(BLOCKS)]
        left = [west[part]] + blocks[:-1]
        right = blocks[1:] + [east[part]]
        for k in range(BLOCKS):
            shifted = [
                jnp.where(lane == 0, pltpu.roll(left[k], 1, 1), pltpu.roll(blocks[k], 1, 1)),
                blocks[k],
                jnp.where(lane == 127, pltpu.roll(right[k], 127, 1), pltpu.roll(blocks[k], 127, 1)),
            ]
            for q in range(3):
                plane = part * 3 + q
                table[plane, k] = shifted[q]
                first_edge[plane, k] = shifted[q][0:1]
                last_edge[plane, k] = shifted[q][ROWS - 1 : ROWS]


def node_table(velocity, west, east):
    vmem = pl.BlockSpec(memory_space=pltpu.VMEM)
    return pl.pallas_call(
        table_kernel,
        out_shape=[
            jax.ShapeDtypeStruct((6, BLOCKS, ROWS, 128), f32),
            jax.ShapeDtypeStruct((6, BLOCKS, 1, 128), f32),
            jax.ShapeDtypeStruct((6, BLOCKS, 1, 128), f32),
        ],
        in_specs=[vmem] * 3,
        out_specs=[vmem] * 3,
        name="table",
    )(velocity, west, east)


def spline(frac):
    lower = 0.5 * (0.5 - frac) * (0.5 - frac)
    middle = 0.75 - frac * frac
    upper = 0.5 * (0.5 + frac) * (0.5 + frac)
    return (lower, middle, upper)


def transfer_kernel(
    first, last, spans, counts,
    table, above, below, near, frac, index, words,
    state, north, south, east, west,
    nodes, samples, columns, buffer,
):
    nodes[6 * PLANE : 8 * PLANE, :] = jnp.zeros((2 * PLANE, 128), f32)
    for plane in range(6):
        for k in range(BLOCKS):
            base = plane * PLANE + k * PAD_ROWS
            nodes[base + 8 : base + 8 + ROWS, :] = table[plane, k]
            nodes[base + 7 : base + 8, :] = above[plane, k]
            nodes[base + 8 + ROWS : base + 9 + ROWS, :] = below[plane, k]

    def group(v, carry):
        def chunk(step, sums):
            sums = list(sums)
            for s in range(8):
                block = v * 8 + s
                here = jnp.minimum(first[block] + step, last[block])
                base = here + lax.shift_right_logical(here, 7) * 16 + 8
                spot = near[pl.ds(block, 8, stride=0), :]
                lanes = spot & 127
                inside = lax.shift_right_logical(spot, 7) == here
                for r in range(3):
                    got = from_lanes(nodes[pl.ds(base + r - 1, 8, stride=PLANE), :], lanes)
                    sums[3 * s + r] = jnp.where(inside, got, sums[3 * s + r])
            return tuple(sums)

        sums = lax.fori_loop(0, spans[v], chunk, tuple(jnp.zeros((8, 128), f32) for _ in range(24)))
        for s in range(8):
            for r in range(3):
                samples[pl.ds(r * 2048 + v * 8 + s, 8, stride=256), :] = sums[3 * s + r]
        here = pl.ds(pl.multiple_of(v * 8, 8), 8)
        d_row = frac[0, v]
        d_col = frac[1, v]
        w_row = spline(d_row)
        w_col = spline(d_col)
        arm_row = [4.0 * w_row[r] * (r - 1 - d_row) for r in range(3)]
        arm_col = [4.0 * w_col[q] * (q - 1 - d_col) for q in range(3)]
        speeds = []
        affines = []
        for part in range(2):
            speed = along_row = along_col = None
            for q in range(3):
                plane = part * 3 + q
                got = [
                    samples[pl.ds(pl.multiple_of(r * 2048 + plane * 256 + v * 8, 8), 8), :]
                    for r in range(3)
                ]
                plain = w_row[0] * got[0] + w_row[1] * got[1] + w_row[2] * got[2]
                tilted = arm_row[0] * got[0] + arm_row[1] * got[1] + arm_row[2] * got[2]
                terms = (w_col[q] * plain, w_col[q] * tilted, arm_col[q] * plain)
                if q == 0:
                    speed, along_row, along_col = terms
                else:
                    speed = speed + terms[0]
                    along_row = along_row + terms[1]
                    along_col = along_col + terms[2]
            speeds.append(speed)
            affines += [along_row, along_col]
        values = [d_row + step_dt * speeds[0], d_col + step_dt * speeds[1]] + speeds + affines
        for c in range(8):
            state[c, v] = values[c]
        return carry

    lax.fori_loop(0, VREGS, group, 0)

    direction = lax.shift_right_logical(sublane_ids(), 1)
    count = jnp.where(
        direction < 2,
        jnp.where(direction == 0, counts[0], counts[1]),
        jnp.where(direction == 2, counts[2], counts[3]),
    )
    slot = (sublane_ids() & 1) * 4096 + lane_ids()

    def finish(v, moved):
        kept = slot + v * 128 < count
        for c in range(8):
            columns[pl.ds(v * 8 + c, 8, stride=256), :] = jnp.where(kept, moved[c], 0.0)

    apply_network(
        8, lambda c, v: state[c, v], buffer, index.at[0], words.at[0, 0], words.at[0, 1], finish
    )
    for k, out in enumerate((north, south, east, west)):
        for j in range(64):
            base = (k * 64 + j) * 8
            out[:, 128 * j : 128 * j + 128] = columns[base : base + 8, :]


def transfer(bounds, spans, counts, table, above, below, near, frac, index, words):
    vmem = pl.BlockSpec(memory_space=pltpu.VMEM)
    smem = pl.BlockSpec(memory_space=pltpu.SMEM)
    return pl.pallas_call(
        transfer_kernel,
        out_shape=[jax.ShapeDtypeStruct((8, VREGS, 8, 128), f32)]
        + [jax.ShapeDtypeStruct((8, CAP), f32)] * 4,
        in_specs=[smem] * 4 + [vmem] * 7,
        out_specs=[vmem] * 5,
        scratch_shapes=[
            pltpu.VMEM((8 * PLANE, 128), f32),
            pltpu.VMEM((3 * 2048, 128), f32),
            pltpu.VMEM((2048, 128), f32),
            pltpu.VMEM((8, VREGS, 8, 128), f32),
        ],
        compiler_params=pltpu.CompilerParams(vmem_limit_bytes=40 << 20),
        cost_estimate=pl.CostEstimate(flops=20_000_000, bytes_accessed=8_000_000, transcendentals=0),
        name="transfer",
    )(bounds[0], bounds[1], spans, counts, table, above, below, near.reshape(256, 128), frac, index, words)


def restore_kernel(state, offsets, index, words, out, columns, buffer):
    def finish(v, moved):
        for c in range(2):
            frac = offsets[pl.ds(c * 256 + v, 8, stride=32), :]
            columns[pl.ds(v * 8 + c, 8, stride=256), :] = frac + step_dt * moved[c]
        for c in range(6):
            columns[pl.ds(v * 8 + c + 2, 8, stride=256), :] = moved[c]

    apply_network(
        6, lambda c, v: state[c + 2, v], buffer, index.at[1], words.at[1, 0], words.at[1, 1], finish
    )
    for j in range(256):
        out[:, 128 * j : 128 * j + 128] = columns[8 * j : 8 * j + 8, :]


def restore(state, offsets, index, words):
    vmem = pl.BlockSpec(memory_space=pltpu.VMEM)
    return pl.pallas_call(
        restore_kernel,
        out_shape=jax.ShapeDtypeStruct((8, 4 * CAP), f32),
        in_specs=[vmem] * 4,
        out_specs=vmem,
        scratch_shapes=[pltpu.VMEM((2048, 128), f32), pltpu.VMEM((6, VREGS, 8, 128), f32)],
        compiler_params=pltpu.CompilerParams(vmem_limit_bytes=32 << 20),
        cost_estimate=pl.CostEstimate(flops=10_000_000, bytes_accessed=4_000_000, transcendentals=0),
        name="restore",
    )(state, offsets.reshape(512, 128), index, words)


def from_behind(block, axis, distance):
    devices = range(lax.axis_size(axis))
    route = [(i - distance, i) for i in devices if i - distance in devices]
    return lax.ppermute(block, axis, route)


def passed_along(value, axis, by):
    count = lax.axis_size(axis)
    return lax.ppermute(value, axis, [(i, (i + by) % count) for i in range(count)])


def shards(ocean, grid_mass, grid_momentum, cells, offsets, moves, slots):
    outgoing = ocean.reshape(4, 8, 16, COLS).transpose(2, 0, 1, 3)
    forcing = lax.all_to_all(outgoing, "lon", 0, 0)
    planned = plan(cells, offsets, moves, slots)
    near, frac, counts, index, words = planned
    ends = lax.shift_right_logical(near.reshape(256, 128), 7)
    bounds = (ends[:, 0], ends[:, 127])
    spans = jnp.max((bounds[1] - bounds[0]).reshape(VREGS, 8), axis=1) + 1
    velocity = node_velocity(forcing, grid_mass, grid_momentum)
    west = passed_along(velocity[:, :, COLS - 128 :], "lon", 1)
    east = passed_along(velocity[:, :, :128], "lon", -1)
    table, first_edge, last_edge = node_table(velocity, west, east)
    above = from_behind(last_edge, "lat", 1)
    below = from_behind(first_edge, "lat", -1)
    state, north, south, east, west = transfer(
        bounds, spans, counts, table, above, below, near, frac, index, words
    )
    north = from_behind(north, "lat", 1)
    south = from_behind(south, "lat", -1)
    east = passed_along(east, "lon", 1)
    west = passed_along(west, "lon", -1)
    parcels = restore(state, offsets, index, words)
    return (parcels, jnp.concatenate([north, south, east, west], axis=1))


def solution(mesh):
    in_specs = (
        P(None, ("lat", "lon"), None),
        P("lat", "lon"),
        P(None, "lat", "lon"),
        P(("lat", "lon")),
        P(None, ("lat", "lon")),
        P(("lat", "lon")),
        P(("lat", "lon")),
    )
    out_specs = (P(None, ("lat", "lon")), P(None, ("lat", "lon")))
    return jax.shard_map(shards, mesh=mesh, in_specs=in_specs, out_specs=out_specs, check_vma=False)
```

```python
import jax
import jax.numpy as jnp
from jax import lax
from jax.experimental import pallas as pl
from jax.experimental.pallas import tpu as pltpu
from jax.sharding import PartitionSpec as P

CAP = 8192
ROWS = 128
COLS = 384
BLOCKS = 3
VREGS = 32
PLANE = BLOCKS * ROWS
EDGE_PLANE = PLANE + 32
LON = 16

step_dt = 0.5
drag_coef = 2.0

f32 = jnp.float32
i32 = jnp.int32


def lane_ids():
    return lax.broadcasted_iota(i32, (8, 128), 1)


def sublane_ids():
    return lax.broadcasted_iota(i32, (8, 128), 0)


def from_lanes(x, index):
    return jnp.take_along_axis(x, index, axis=1, mode="promise_in_bounds")


def from_sublanes(x, index):
    return jnp.take_along_axis(x, index, axis=0, mode="promise_in_bounds")


def bit_set(words, place):
    return lax.shift_left(words, 31 - place) < 0


def lane_pass(xs, distance_bit, uppers, perm):
    out = []
    for v, x in enumerate(xs):
        other = from_lanes(x, perm)
        out.append(
            jnp.where(uppers[v % len(uppers)], jnp.maximum(x, other), jnp.minimum(x, other))
        )
    return out


def lane_bit(k):
    return lax.shift_right_logical(lane_ids(), k) & 1


def lane_passes(xs, top, flips):
    lane = lane_ids()
    for j in range(top, -1, -1):
        uppers = [(lane_bit(j) ^ flip) != 0 for flip in flips]
        xs = lane_pass(xs, j, uppers, lane ^ (1 << j))
    return xs


def sort_network(keys, payloads, record):
    lane = lane_ids()
    lane_f = lane.astype(f32)
    sub = sublane_ids()
    words = [jnp.zeros((8, 128), i32) for _ in range(VREGS)] if record else None
    sub_words = [jnp.zeros((8, 128), i32) for _ in range(VREGS)] if record else None

    xs = [key * 128.0 + lane_f for key in keys]
    for k in range(1, 7):
        xs = lane_passes(xs, k - 1, (lane_bit(k),))
    xs = lane_passes(xs, 6, (0, 1))

    def settle(t, xs):
        out = []
        for v in range(VREGS):
            index = xs[v].astype(i32) & 127
            if record:
                record(t, v, index)
            for payload in payloads:
                payload[v] = from_lanes(payload[v], index)
            out.append(xs[v] - index.astype(f32) + lane_f)
        return out

    xs = settle(0, xs)
    for t in range(1, 9):
        sign = None
        if 5 <= t <= 7:
            sign = jnp.where((lax.shift_right_logical(sub, t - 5) & 1) != 0, -1.0, 1.0)
            xs = [x * sign for x in xs]
        for i in range(t - 1, -1, -1):
            if i >= 5:
                near = i - 5
                perm = sub ^ (1 << near)
                upper = (lax.shift_right_logical(sub, near) & 1) != 0
                for v in range(VREGS):
                    x = xs[v]
                    other = from_sublanes(x, perm)
                    take = jnp.where(upper, other, x) > jnp.where(upper, x, other)
                    xs[v] = jnp.where(take, other, x)
                    if record:
                        sub_words[v] = sub_words[v] | jnp.where(take, 1 << sub_place(t, i), 0)
                    for payload in payloads:
                        y = payload[v]
                        payload[v] = jnp.where(take, from_sublanes(y, perm), y)
            else:
                for a in range(VREGS):
                    if a & (1 << i):
                        continue
                    b = a | (1 << i)
                    x, y = xs[a], xs[b]
                    down = t <= 4 and (a >> t) & 1
                    swap = x < y if down else x > y
                    low, high = jnp.minimum(x, y), jnp.maximum(x, y)
                    xs[a], xs[b] = (high, low) if down else (low, high)
                    if record:
                        words[a] = words[a] | jnp.where(swap, 1 << row_place(t, i), 0)
                    for payload in payloads:
                        x, y = payload[a], payload[b]
                        payload[a] = jnp.where(swap, y, x)
                        payload[b] = jnp.where(swap, x, y)
        if t <= 4:
            runs = [xs[v] for v in range(VREGS)]
            lane_done = []
            ups = [v for v in range(VREGS) if not (v >> t) & 1]
            downs = [v for v in range(VREGS) if (v >> t) & 1]
            up_x = lane_passes([runs[v] for v in ups], 6, (0,))
            down_x = lane_passes([runs[v] for v in downs], 6, (1,)) if downs else []
            for v, x in zip(ups, up_x):
                xs[v] = x
            for v, x in zip(downs, down_x):
                xs[v] = x
        else:
            xs = lane_passes(xs, 6, (0,))
            if sign is not None:
                xs = [x * sign for x in xs]
        xs = settle(t, xs)
    return xs, words, sub_words


def row_place(t, i):
    return t * (t - 1) // 2 + t - 1 - i if t <= 5 else 5 * t - 15 + 4 - i


def sub_place(t, i):
    return {6: 0, 7: 1, 8: 3}[t] + t - 1 - i


def apply_network(count, source, buffer, index, words, sub_words, finish):
    sub = sublane_ids()
    for v in range(VREGS):
        lanes = index[0, v]
        for c in range(count):
            buffer[c, v] = from_lanes(source(c, v), lanes)
    for t in range(1, 9):
        steps = [i for i in range(t - 1, -1, -1) if i >= 5]
        if steps:
            for v in range(VREGS):
                takes = [bit_set(sub_words[v], sub_place(t, i)) for i in steps]
                for c in range(count):
                    x = buffer[c, v]
                    for i, take in zip(steps, takes):
                        x = jnp.where(take, from_sublanes(x, sub ^ (1 << (i - 5))), x)
                    buffer[c, v] = x
        top = min(t, 5)
        rounds = {1: ((0,),), 2: ((1, 0),), 3: ((2, 1, 0),), 4: ((3, 2), (1, 0)), 5: ((4, 3), (2, 1, 0))}[top]
        for bits in rounds:
            mask = sum(1 << i for i in bits)
            for base in range(VREGS):
                if base & mask:
                    continue
                members = [v for v in range(VREGS) if v & ~mask == base]
                swaps = {}
                for i in bits:
                    for a in members:
                        if not a & (1 << i):
                            swaps[i, a] = bit_set(words[a], row_place(t, i))
                for c in range(count):
                    xs = {v: buffer[c, v] for v in members}
                    for i in bits:
                        for a in members:
                            if a & (1 << i):
                                continue
                            b = a | (1 << i)
                            x, y = xs[a], xs[b]
                            xs[a] = jnp.where(swaps[i, a], y, x)
                            xs[b] = jnp.where(swaps[i, a], x, y)
                    for v in members:
                        buffer[c, v] = xs[v]
        for v in range(VREGS):
            lanes = index[t, v]
            moved = [from_lanes(buffer[c, v], lanes) for c in range(count)]
            if t < 8:
                for c in range(count):
                    buffer[c, v] = moved[c]
            else:
                finish(v, moved)


def plan_kernel(
    cells, offsets, moves, slots,
    near_out, ends_out, frac_out, counts_out,
    index_out, words_out,
    tags, chunks,
):
    lane = lane_ids()
    sub = sublane_ids()
    stay = jnp.where(moves[...] == 0, 1.0, 0.0)
    before = jnp.where(
        lax.broadcasted_iota(i32, (128, 128), 0) < lax.broadcasted_iota(i32, (128, 128), 1), 1.0, 0.0
    )
    rank = jnp.dot(stay, before, preferred_element_type=f32)
    above = jnp.where(
        lax.broadcasted_iota(i32, (256, 256), 1) < lax.broadcasted_iota(i32, (256, 256), 0), 1.0, 0.0
    )
    totals = jnp.broadcast_to(jnp.sum(stay, axis=1, keepdims=True), (256, 128))
    rank = rank + jnp.dot(above, totals, preferred_element_type=f32)
    rank = rank.astype(i32)
    counts = []
    for k in range(4):
        count = jnp.sum(jnp.where(moves[...] == k + 1, 1.0, 0.0)).astype(i32)
        counts.append(count)
        counts_out[k] = count
    hole = rank + counts[0]
    filled = counts[0]
    for k in range(1, 4):
        hole = hole + jnp.where(rank >= k * CAP - filled, counts[k], 0)
        filled = filled + counts[k]
    target = jnp.where(moves[...] > 0, (moves[...] - 1) * CAP + slots[...], hole)
    number = lax.broadcasted_iota(i32, (256, 128), 0) * 128 + lax.broadcasted_iota(i32, (256, 128), 1)
    cell = cells[...]
    row = (cell.astype(f32) * (1.0 / COLS)).astype(i32)
    row = row - jnp.where(row * COLS > cell, 1, 0)
    row = row + jnp.where((row + 1) * COLS <= cell, 1, 0)
    col = cell - row * COLS
    part = lax.shift_right_logical(col, 7)
    edge = jnp.where(row == 0, 0, 1)
    inner = (row > 0) & (row < ROWS - 1)
    spot = jnp.where(inner, 8 + part * ROWS + row, 2 * part + edge) * 128 + (col & 127)
    keys = []
    for v in range(VREGS):
        part = slice(v * 8, v * 8 + 8)
        keys.append(spot[part].astype(f32))
        tags[v] = lax.shift_left(target[part], 15) | number[part]
        frac_out[0, v] = offsets[0, part]
        frac_out[1, v] = offsets[1, part]
    keys, _, _ = sort_network(keys, (frac_out.at[0], frac_out.at[1], tags), None)
    for v in range(VREGS):
        spots = lax.shift_right_logical(keys[v].astype(i32), 7)
        near_out[v] = spots
        chunks[v * 8 : v * 8 + 8, :] = lax.shift_right_logical(spots, 7).astype(f32)
    for half in range(2):
        turned = jnp.transpose(chunks[half * 128 : half * 128 + 128, :]).astype(i32)
        ends_out[half : half + 1, :] = turned[0:1]
        ends_out[half + 2 : half + 3, :] = turned[127:128]

    def one(which, carry):
        keys = [
            (lax.shift_right_logical(tags[v], jnp.where(which == 0, 15, 0)) & 32767).astype(f32)
            for v in range(VREGS)
        ]

        def record(t, v, index):
            index_out[which, t, v] = index

        _, words, sub_words = sort_network(keys, (), record)
        for v in range(VREGS):
            words_out[which, 0, v] = words[v]
            words_out[which, 1, v] = sub_words[v]
        return carry

    lax.fori_loop(0, 2, one, 0)


def plan(cells, offsets, moves, slots):
    vmem = pl.BlockSpec(memory_space=pltpu.VMEM)
    smem = pl.BlockSpec(memory_space=pltpu.SMEM)
    return pl.pallas_call(
        plan_kernel,
        out_shape=[
            jax.ShapeDtypeStruct((VREGS, 8, 128), i32),
            jax.ShapeDtypeStruct((4, 128), i32),
            jax.ShapeDtypeStruct((2, VREGS, 8, 128), f32),
            jax.ShapeDtypeStruct((4,), i32),
            jax.ShapeDtypeStruct((2, 9, VREGS, 8, 128), i32),
            jax.ShapeDtypeStruct((2, 2, VREGS, 8, 128), i32),
        ],
        in_specs=[vmem] * 4,
        out_specs=[vmem, vmem, vmem, smem, vmem, vmem],
        scratch_shapes=[pltpu.VMEM((VREGS, 8, 128), i32), pltpu.VMEM((256, 128), f32)],
        compiler_params=pltpu.CompilerParams(vmem_limit_bytes=32 << 20),
        cost_estimate=pl.CostEstimate(flops=20_000_000, bytes_accessed=8_000_000, transcendentals=0),
        name="plan",
    )(cells.reshape(256, 128), offsets.reshape(2, 256, 128), moves.reshape(256, 128), slots.reshape(256, 128))


def pack_kernel(ocean, mass, momentum, out, last, first):
    lane = lax.broadcasted_iota(i32, (8, 128), 1)
    tiles = LON * BLOCKS

    def tile(part, k):
        k = k % tiles
        return ocean[part, :, 128 * k : 128 * k + 128]

    spots = (0, 1, 4, 5)
    for b in range(LON):
        rim = jnp.zeros((8, 128), f32)
        for part in range(4):
            for k in range(BLOCKS):
                column = (part * BLOCKS + k) * 128
                out[b, :, column : column + 128] = tile(part, BLOCKS * b + k)
            spot = spots[part]
            rim = jnp.where(lane == spot, pltpu.roll(tile(part, BLOCKS * b - 1), spot + 1, 1), rim)
            rim = jnp.where(lane == spot + 2, pltpu.roll(tile(part, BLOCKS * b + BLOCKS), spot + 2, 1), rim)
        out[b, :, 4 * COLS : 4 * COLS + 128] = rim
    lanes = lax.broadcasted_iota(i32, (ROWS, 128), 1)
    for side, out_side in ((0, last), (1, first)):
        column = 0 if side else COLS - 128
        sources = [mass[:, column : column + 128]] * 2 + [
            momentum[part, :, column : column + 128] for part in range(2)
        ]
        rim = jnp.ones((ROWS, 128), f32)
        for source, spot in zip(sources, spots):
            spot = spot + 2 * side
            shift = spot if side else spot + 1
            rim = jnp.where(lanes == spot, pltpu.roll(source, shift, 1), rim)
        out_side[...] = rim


def pack(ocean, mass, momentum):
    vmem = pl.BlockSpec(memory_space=pltpu.VMEM)
    return pl.pallas_call(
        pack_kernel,
        out_shape=[
            jax.ShapeDtypeStruct((LON, 8, 4 * COLS + 128), f32),
            jax.ShapeDtypeStruct((ROWS, 128), f32),
            jax.ShapeDtypeStruct((ROWS, 128), f32),
        ],
        in_specs=[vmem] * 3,
        out_specs=[vmem] * 3,
        name="pack",
    )(ocean, mass, momentum)


def drive(momentum, stress, mass, current):
    return (momentum + step_dt * stress + step_dt * drag_coef * mass * current) / (
        mass * (1.0 + step_dt * drag_coef)
    )


def table_kernel(forcing, mass, momentum, west, east, table, first_edge, last_edge):
    lane = lax.broadcasted_iota(i32, (ROWS, 128), 1)
    rim = forcing[:, :, 4 * COLS : 4 * COLS + 128].reshape(ROWS, 128)
    beside = jnp.where((lane & 2) == 0, west[...], east[...])
    rim = drive(pltpu.roll(beside, 124, 1), pltpu.roll(rim, 124, 1), beside, rim)
    for part in range(2):
        blocks, after, before = [], [], []
        for k in range(BLOCKS):
            column = 128 * k
            current = forcing[:, :, COLS * part + column : COLS * part + column + 128]
            stress = forcing[:, :, COLS * (2 + part) + column : COLS * (2 + part) + column + 128]
            block = drive(
                momentum[part, :, column : column + 128],
                stress.reshape(ROWS, 128),
                mass[:, column : column + 128],
                current.reshape(ROWS, 128),
            )
            blocks.append(block)
            after.append(pltpu.roll(block, 1, 1))
            before.append(pltpu.roll(block, 127, 1))
        left = [pltpu.roll(rim, 127, 1) if part else rim] + after[:-1]
        right = before[1:] + [pltpu.roll(rim, 125 - part, 1)]
        for k in range(BLOCKS):
            shifted = (
                jnp.where(lane == 0, left[k], after[k]),
                blocks[k],
                jnp.where(lane == 127, right[k], before[k]),
            )
            for q in range(3):
                plane = part * 3 + q
                spot = plane * BLOCKS + k
                table[plane, ROWS * k : ROWS * k + ROWS, :] = shifted[q]
                first_edge[spot : spot + 1, :] = shifted[q][0:1]
                last_edge[spot : spot + 1, :] = shifted[q][ROWS - 1 : ROWS]
    for plane in (6, 7):
        table[plane] = jnp.zeros((PLANE, 128), f32)
    first_edge[18:24, :] = jnp.zeros((6, 128), f32)
    last_edge[18:24, :] = jnp.zeros((6, 128), f32)


def node_table(forcing, mass, momentum, west, east):
    vmem = pl.BlockSpec(memory_space=pltpu.VMEM)
    return pl.pallas_call(
        table_kernel,
        out_shape=[
            jax.ShapeDtypeStruct((8, PLANE, 128), f32),
            jax.ShapeDtypeStruct((24, 128), f32),
            jax.ShapeDtypeStruct((24, 128), f32),
        ],
        in_specs=[vmem] * 5,
        out_specs=[vmem] * 3,
        name="table",
    )(forcing, mass, momentum, west, east)


def spline(frac):
    lower = 0.5 * (0.5 - frac) * (0.5 - frac)
    middle = 0.75 - frac * frac
    upper = 0.5 * (0.5 + frac) * (0.5 + frac)
    return (lower, middle, upper)


def interpolate_group(g, ends, near, frac, nodes, stride, address, samples, state):
    high = lax.shift_right_logical(g & 3, 1)
    low = (g & 1) * 64 + lax.shift_right_logical(g, 2)
    start = (g & 3) * 64 + lax.shift_right_logical(g, 2)
    first = [ends[high, low + 8 * j] for j in range(8)]
    last = [ends[high + 2, low + 8 * j] for j in range(8)]
    span = last[0] - first[0]
    for j in range(1, 8):
        span = jnp.maximum(span, last[j] - first[j])

    def trip(step, sums):
        sums = list(sums)
        for j in range(8):
            spot = near[pl.ds(start + 8 * j, 8, stride=0), :]
            lanes = spot & 127
            chunk = lax.shift_right_logical(spot, 7)
            for more in range(2):
                here = jnp.minimum(first[j] + 2 * step + more, last[j])
                base = address(here)
                inside = chunk == here
                for r in range(3):
                    got = from_lanes(nodes[pl.ds(base + r - 1, 8, stride=stride), :], lanes)
                    sums[3 * j + r] = jnp.where(inside, got, sums[3 * j + r])
        return tuple(sums)

    trips = lax.shift_right_logical(span, 1) + 1
    sums = lax.fori_loop(0, trips, trip, tuple(jnp.zeros((8, 128), f32) for _ in range(24)))
    for j in range(8):
        for r in range(3):
            samples[pl.ds(r * 64 + j, 8, stride=8), :] = sums[3 * j + r]
    rows = pl.ds(start, 8, stride=8)
    d_row = frac[0, rows, :]
    d_col = frac[1, rows, :]
    w_row = spline(d_row)
    w_col = spline(d_col)
    arm_row = [4.0 * w_row[r] * (r - 1 - d_row) for r in range(3)]
    arm_col = [4.0 * w_col[q] * (q - 1 - d_col) for q in range(3)]
    speeds = []
    affines = []
    for part in range(2):
        speed = along_row = along_col = None
        for q in range(3):
            plane = part * 3 + q
            got = [samples[r * 64 + plane * 8 : r * 64 + plane * 8 + 8, :] for r in range(3)]
            plain = w_row[0] * got[0] + w_row[1] * got[1] + w_row[2] * got[2]
            tilted = arm_row[0] * got[0] + arm_row[1] * got[1] + arm_row[2] * got[2]
            terms = (w_col[q] * plain, w_col[q] * tilted, arm_col[q] * plain)
            if q == 0:
                speed, along_row, along_col = terms
            else:
                speed = speed + terms[0]
                along_row = along_row + terms[1]
                along_col = along_col + terms[2]
        speeds.append(speed)
        affines += [along_row, along_col]
    values = [d_row + step_dt * speeds[0], d_col + step_dt * speeds[1]] + speeds + affines
    for c in range(8):
        state[c, rows, :] = values[c]


def group_first(g, ends):
    return ends[lax.shift_right_logical(g & 3, 1), (g & 1) * 64 + lax.shift_right_logical(g, 2)]


def inner_kernel(ends, table, near, frac, state, samples):
    def group(g, carry):
        @pl.when(group_first(g, ends) >= 8)
        def _():
            interpolate_group(
                g, ends, near, frac, table, PLANE, lambda chunk: chunk - 8, samples, state
            )

        return carry

    lax.fori_loop(0, VREGS, group, 0)


def inner(ends, table, near, frac):
    vmem = pl.BlockSpec(memory_space=pltpu.VMEM)
    smem = pl.BlockSpec(memory_space=pltpu.SMEM)
    return pl.pallas_call(
        inner_kernel,
        out_shape=jax.ShapeDtypeStruct((8, 256, 128), f32),
        in_specs=[smem] + [vmem] * 3,
        out_specs=vmem,
        scratch_shapes=[pltpu.VMEM((192, 128), f32)],
        compiler_params=pltpu.CompilerParams(vmem_limit_bytes=24 << 20),
        cost_estimate=pl.CostEstimate(flops=20_000_000, bytes_accessed=8_000_000, transcendentals=0),
        name="inner",
    )(ends, table.reshape(8 * PLANE, 128), near.reshape(256, 128), frac.reshape(2, 256, 128))


def transfer_kernel(
    ends, counts,
    table, above, below, near, frac, early, index, words,
    state, north, south, east, west,
    nodes, samples, columns, buffer,
):
    for c in range(8):
        state[c] = early[c]
    for plane in range(6):
        base = plane * EDGE_PLANE
        nodes[base : base + PLANE, :] = table[plane]
        for k in range(BLOCKS):
            spot = plane * BLOCKS + k
            edge = base + PLANE + 8 * k
            top = k * ROWS
            nodes[edge : edge + 1, :] = above[spot : spot + 1, :]
            nodes[edge + 1 : edge + 3, :] = table[plane, top : top + 2, :]
            nodes[edge + 4 : edge + 6, :] = table[plane, top + ROWS - 2 : top + ROWS, :]
            nodes[edge + 6 : edge + 7, :] = below[spot : spot + 1, :]
    nodes[6 * EDGE_PLANE : 8 * EDGE_PLANE, :] = jnp.zeros((2 * EDGE_PLANE, 128), f32)

    def address(chunk):
        return jnp.where(chunk < 8, PLANE + 1 + 4 * chunk, jnp.maximum(chunk - 8, 1))

    def group(g, carry):
        @pl.when(group_first(g, ends) < 8)
        def _():
            interpolate_group(g, ends, near, frac, nodes, EDGE_PLANE, address, samples, state)

        return carry

    lax.fori_loop(0, VREGS, group, 0)

    direction = lax.shift_right_logical(sublane_ids(), 1)
    count = jnp.where(
        direction < 2,
        jnp.where(direction == 0, counts[0], counts[1]),
        jnp.where(direction == 2, counts[2], counts[3]),
    )
    slot = (sublane_ids() & 1) * 4096 + lane_ids()

    def finish(v, moved):
        kept = slot + v * 128 < count
        for c in range(8):
            columns[pl.ds(v * 8 + c, 8, stride=256), :] = jnp.where(kept, moved[c], 0.0)

    apply_network(
        8,
        lambda c, v: state[c, 8 * v : 8 * v + 8, :],
        buffer, index.at[0], words.at[0, 0], words.at[0, 1], finish,
    )
    for k, out in enumerate((north, south, east, west)):
        for j in range(64):
            base = (k * 64 + j) * 8
            out[:, 128 * j : 128 * j + 128] = columns[base : base + 8, :]


def transfer(ends, counts, table, above, below, near, frac, early, index, words):
    vmem = pl.BlockSpec(memory_space=pltpu.VMEM)
    smem = pl.BlockSpec(memory_space=pltpu.SMEM)
    return pl.pallas_call(
        transfer_kernel,
        out_shape=[jax.ShapeDtypeStruct((8, 256, 128), f32)]
        + [jax.ShapeDtypeStruct((8, CAP), f32)] * 4,
        in_specs=[smem] * 2 + [vmem] * 8,
        out_specs=[vmem] * 5,
        scratch_shapes=[
            pltpu.VMEM((8 * EDGE_PLANE, 128), f32),
            pltpu.VMEM((192, 128), f32),
            pltpu.VMEM((2048, 128), f32),
            pltpu.VMEM((8, VREGS, 8, 128), f32),
        ],
        compiler_params=pltpu.CompilerParams(vmem_limit_bytes=32 << 20),
        cost_estimate=pl.CostEstimate(flops=10_000_000, bytes_accessed=8_000_000, transcendentals=0),
        name="transfer",
    )(
        ends, counts, table, above, below,
        near.reshape(256, 128), frac.reshape(2, 256, 128), early, index, words,
    )


def restore_kernel(state, offsets, index, words, out, columns, buffer):
    def finish(v, moved):
        for c in range(2):
            frac = offsets[pl.ds(c * 256 + v, 8, stride=32), :]
            columns[pl.ds(v * 8 + c, 8, stride=256), :] = frac + step_dt * moved[c]
        for c in range(6):
            columns[pl.ds(v * 8 + c + 2, 8, stride=256), :] = moved[c]

    apply_network(
        6,
        lambda c, v: state[c + 2, 8 * v : 8 * v + 8, :],
        buffer, index.at[1], words.at[1, 0], words.at[1, 1], finish,
    )
    for j in range(256):
        out[:, 128 * j : 128 * j + 128] = columns[8 * j : 8 * j + 8, :]


def restore(state, offsets, index, words):
    vmem = pl.BlockSpec(memory_space=pltpu.VMEM)
    return pl.pallas_call(
        restore_kernel,
        out_shape=jax.ShapeDtypeStruct((8, 4 * CAP), f32),
        in_specs=[vmem] * 4,
        out_specs=vmem,
        scratch_shapes=[pltpu.VMEM((2048, 128), f32), pltpu.VMEM((6, VREGS, 8, 128), f32)],
        compiler_params=pltpu.CompilerParams(vmem_limit_bytes=32 << 20),
        cost_estimate=pl.CostEstimate(flops=10_000_000, bytes_accessed=4_000_000, transcendentals=0),
        name="restore",
    )(state, offsets.reshape(512, 128), index, words)


def from_behind(block, axis, distance):
    devices = range(lax.axis_size(axis))
    route = [(i - distance, i) for i in devices if i - distance in devices]
    return lax.ppermute(block, axis, route)


def passed_along(value, axis, by):
    count = lax.axis_size(axis)
    return lax.ppermute(value, axis, [(i, (i + by) % count) for i in range(count)])


def shards(ocean, grid_mass, grid_momentum, cells, offsets, moves, slots):
    outgoing, last, first = pack(ocean, grid_mass, grid_momentum)
    forcing = lax.all_to_all(outgoing, "lon", 0, 0)
    west = passed_along(last, "lon", 1)
    east = passed_along(first, "lon", -1)
    near, ends, frac, counts, index, words = plan(cells, offsets, moves, slots)
    forcing, near = lax.optimization_barrier((forcing, near))
    table, first_edge, last_edge = node_table(forcing, grid_mass, grid_momentum, west, east)
    above = from_behind(last_edge, "lat", 1)
    below = from_behind(first_edge, "lat", -1)
    early = inner(ends, table, near, frac)
    state, north, south, east, west = transfer(
        ends, counts, table, above, below, near, frac, early, index, words
    )
    north = from_behind(north, "lat", 1)
    south = from_behind(south, "lat", -1)
    east = passed_along(east, "lon", 1)
    west = passed_along(west, "lon", -1)
    parcels = restore(state, offsets, index, words)
    return (parcels, jnp.concatenate([north, south, east, west], axis=1))


def solution(mesh):
    in_specs = (
        P(None, ("lat", "lon"), None),
        P("lat", "lon"),
        P(None, "lat", "lon"),
        P(("lat", "lon")),
        P(None, ("lat", "lon")),
        P(("lat", "lon")),
        P(("lat", "lon")),
    )
    out_specs = (P(None, ("lat", "lon")), P(None, ("lat", "lon")))
    return jax.shard_map(shards, mesh=mesh, in_specs=in_specs, out_specs=out_specs, check_vma=False)
```

```python
import jax
import jax.numpy as jnp
from jax import lax
from jax.experimental import pallas as pl
from jax.experimental.pallas import tpu as pltpu
from jax.sharding import PartitionSpec as P

CAP = 8192
ROWS = 128
COLS = 384
BLOCKS = 3
VREGS = 32
PLANE = BLOCKS * ROWS
EDGE_PLANE = PLANE + 32
LON = 16

step_dt = 0.5
drag_coef = 2.0

f32 = jnp.float32
i32 = jnp.int32


def lane_ids():
    return lax.broadcasted_iota(i32, (8, 128), 1)


def sublane_ids():
    return lax.broadcasted_iota(i32, (8, 128), 0)


def from_lanes(x, index):
    return jnp.take_along_axis(x, index, axis=1, mode="promise_in_bounds")


def from_sublanes(x, index):
    return jnp.take_along_axis(x, index, axis=0, mode="promise_in_bounds")


def bit_set(words, place):
    return lax.shift_left(words, 31 - place) < 0


def lane_pass(xs, distance_bit, uppers, perm):
    out = []
    for v, x in enumerate(xs):
        other = from_lanes(x, perm)
        out.append(
            jnp.where(uppers[v % len(uppers)], jnp.maximum(x, other), jnp.minimum(x, other))
        )
    return out


def lane_bit(k):
    return lax.shift_right_logical(lane_ids(), k) & 1


def lane_passes(xs, top, flips):
    lane = lane_ids()
    for j in range(top, -1, -1):
        uppers = [(lane_bit(j) ^ flip) != 0 for flip in flips]
        xs = lane_pass(xs, j, uppers, lane ^ (1 << j))
    return xs


def sort_network(keys, payloads, record):
    lane = lane_ids()
    lane_f = lane.astype(f32)
    sub = sublane_ids()
    words = [jnp.zeros((8, 128), i32) for _ in range(VREGS)] if record else None
    sub_words = [jnp.zeros((8, 128), i32) for _ in range(VREGS)] if record else None

    xs = [key * 128.0 + lane_f for key in keys]
    for k in range(1, 7):
        xs = lane_passes(xs, k - 1, (lane_bit(k),))
    xs = lane_passes(xs, 6, (0, 1))

    def settle(t, xs):
        out = []
        for v in range(VREGS):
            index = xs[v].astype(i32) & 127
            if record:
                record(t, v, index)
            for payload in payloads:
                payload[v] = from_lanes(payload[v], index)
            out.append(xs[v] - index.astype(f32) + lane_f)
        return out

    xs = settle(0, xs)
    for t in range(1, 9):
        sign = None
        if 5 <= t <= 7:
            sign = jnp.where((lax.shift_right_logical(sub, t - 5) & 1) != 0, -1.0, 1.0)
            xs = [x * sign for x in xs]
        for i in range(t - 1, -1, -1):
            if i >= 5:
                near = i - 5
                perm = sub ^ (1 << near)
                upper = (lax.shift_right_logical(sub, near) & 1) != 0
                for v in range(VREGS):
                    x = xs[v]
                    other = from_sublanes(x, perm)
                    take = jnp.where(upper, other, x) > jnp.where(upper, x, other)
                    xs[v] = jnp.where(take, other, x)
                    if record:
                        sub_words[v] = sub_words[v] | jnp.where(take, 1 << sub_place(t, i), 0)
                    for payload in payloads:
                        y = payload[v]
                        payload[v] = jnp.where(take, from_sublanes(y, perm), y)
            else:
                for a in range(VREGS):
                    if a & (1 << i):
                        continue
                    b = a | (1 << i)
                    x, y = xs[a], xs[b]
                    down = t <= 4 and (a >> t) & 1
                    swap = x < y if down else x > y
                    low, high = jnp.minimum(x, y), jnp.maximum(x, y)
                    xs[a], xs[b] = (high, low) if down else (low, high)
                    if record:
                        words[a] = words[a] | jnp.where(swap, 1 << row_place(t, i), 0)
                    for payload in payloads:
                        x, y = payload[a], payload[b]
                        payload[a] = jnp.where(swap, y, x)
                        payload[b] = jnp.where(swap, x, y)
        if t == 8 and not record:
            break
        if t <= 4:
            runs = [xs[v] for v in range(VREGS)]
            lane_done = []
            ups = [v for v in range(VREGS) if not (v >> t) & 1]
            downs = [v for v in range(VREGS) if (v >> t) & 1]
            up_x = lane_passes([runs[v] for v in ups], 6, (0,))
            down_x = lane_passes([runs[v] for v in downs], 6, (1,)) if downs else []
            for v, x in zip(ups, up_x):
                xs[v] = x
            for v, x in zip(downs, down_x):
                xs[v] = x
        else:
            xs = lane_passes(xs, 6, (0,))
            if sign is not None:
                xs = [x * sign for x in xs]
        xs = settle(t, xs)
    return xs, words, sub_words


def row_place(t, i):
    return t * (t - 1) // 2 + t - 1 - i if t <= 5 else 5 * t - 15 + 4 - i


def sub_place(t, i):
    return {6: 0, 7: 1, 8: 3}[t] + t - 1 - i


def apply_network(count, source, buffer, index, words, sub_words, finish):
    sub = sublane_ids()
    for v in range(VREGS):
        lanes = index[0, v]
        for c in range(count):
            buffer[c, v] = from_lanes(source(c, v), lanes)
    for t in range(1, 9):
        steps = [i for i in range(t - 1, -1, -1) if i >= 5]
        if steps:
            for v in range(VREGS):
                takes = [bit_set(sub_words[v], sub_place(t, i)) for i in steps]
                for c in range(count):
                    x = buffer[c, v]
                    for i, take in zip(steps, takes):
                        x = jnp.where(take, from_sublanes(x, sub ^ (1 << (i - 5))), x)
                    buffer[c, v] = x
        top = min(t, 5)
        rounds = {1: ((0,),), 2: ((1, 0),), 3: ((2, 1, 0),), 4: ((3, 2), (1, 0)), 5: ((4, 3), (2, 1, 0))}[top]
        for bits in rounds:
            mask = sum(1 << i for i in bits)
            for base in range(VREGS):
                if base & mask:
                    continue
                members = [v for v in range(VREGS) if v & ~mask == base]
                swaps = {}
                for i in bits:
                    for a in members:
                        if not a & (1 << i):
                            swaps[i, a] = bit_set(words[a], row_place(t, i))
                for c in range(count):
                    xs = {v: buffer[c, v] for v in members}
                    for i in bits:
                        for a in members:
                            if a & (1 << i):
                                continue
                            b = a | (1 << i)
                            x, y = xs[a], xs[b]
                            xs[a] = jnp.where(swaps[i, a], y, x)
                            xs[b] = jnp.where(swaps[i, a], x, y)
                    for v in members:
                        buffer[c, v] = xs[v]
        for v in range(VREGS):
            lanes = index[t, v]
            moved = [from_lanes(buffer[c, v], lanes) for c in range(count)]
            if t < 8:
                for c in range(count):
                    buffer[c, v] = moved[c]
            else:
                finish(v, moved)


def plan_kernel(
    cells, offsets, moves, slots,
    near_out, ends_out, frac_out, counts_out,
    index_out, words_out,
    tags, chunks,
):
    lane = lane_ids()
    sub = sublane_ids()
    stay = jnp.where(moves[...] == 0, 1.0, 0.0)
    before = jnp.where(
        lax.broadcasted_iota(i32, (128, 128), 0) < lax.broadcasted_iota(i32, (128, 128), 1), 1.0, 0.0
    )
    rank = jnp.dot(stay, before, preferred_element_type=f32)
    above = jnp.where(
        lax.broadcasted_iota(i32, (256, 256), 1) < lax.broadcasted_iota(i32, (256, 256), 0), 1.0, 0.0
    )
    totals = jnp.broadcast_to(jnp.sum(stay, axis=1, keepdims=True), (256, 128))
    rank = rank + jnp.dot(above, totals, preferred_element_type=f32)
    rank = rank.astype(i32)
    counts = []
    for k in range(4):
        count = jnp.sum(jnp.where(moves[...] == k + 1, 1.0, 0.0)).astype(i32)
        counts.append(count)
        counts_out[k] = count
    hole = rank + counts[0]
    filled = counts[0]
    for k in range(1, 4):
        hole = hole + jnp.where(rank >= k * CAP - filled, counts[k], 0)
        filled = filled + counts[k]
    target = jnp.where(moves[...] > 0, (moves[...] - 1) * CAP + slots[...], hole)
    number = lax.broadcasted_iota(i32, (256, 128), 0) * 128 + lax.broadcasted_iota(i32, (256, 128), 1)
    cell = cells[...]
    row = (cell.astype(f32) * (1.0 / COLS)).astype(i32)
    row = row - jnp.where(row * COLS > cell, 1, 0)
    row = row + jnp.where((row + 1) * COLS <= cell, 1, 0)
    col = cell - row * COLS
    part = lax.shift_right_logical(col, 7)
    edge = jnp.where(row == 0, 0, 1)
    inner = (row > 0) & (row < ROWS - 1)
    spot = jnp.where(inner, 8 + part * ROWS + row, 2 * part + edge) * 128 + (col & 127)
    keys = []
    for v in range(VREGS):
        part = slice(v * 8, v * 8 + 8)
        keys.append(spot[part].astype(f32))
        tags[v] = lax.shift_left(target[part], 15) | number[part]
        frac_out[0, v] = offsets[0, part]
        frac_out[1, v] = offsets[1, part]
    keys, _, _ = sort_network(keys, (frac_out.at[0], frac_out.at[1], tags), None)
    for v in range(VREGS):
        spots = lax.shift_right_logical(keys[v].astype(i32), 7)
        near_out[v] = spots
        chunks[pl.ds(v, 8, stride=32), :] = lax.shift_right_logical(spots, 7).astype(f32)
    for half in range(2):
        turned = jnp.transpose(chunks[half * 128 : half * 128 + 128, :])
        ends_out[half : half + 1, :] = jnp.min(turned, axis=0, keepdims=True).astype(i32)
        ends_out[half + 2 : half + 3, :] = jnp.max(turned, axis=0, keepdims=True).astype(i32)

    def one(which, carry):
        keys = [
            (lax.shift_right_logical(tags[v], jnp.where(which == 0, 15, 0)) & 32767).astype(f32)
            for v in range(VREGS)
        ]

        def record(t, v, index):
            index_out[which, t, v] = index

        _, words, sub_words = sort_network(keys, (), record)
        for v in range(VREGS):
            words_out[which, 0, v] = words[v]
            words_out[which, 1, v] = sub_words[v]
        return carry

    lax.fori_loop(0, 2, one, 0)


def plan(cells, offsets, moves, slots):
    vmem = pl.BlockSpec(memory_space=pltpu.VMEM)
    smem = pl.BlockSpec(memory_space=pltpu.SMEM)
    return pl.pallas_call(
        plan_kernel,
        out_shape=[
            jax.ShapeDtypeStruct((VREGS, 8, 128), i32),
            jax.ShapeDtypeStruct((4, 128), i32),
            jax.ShapeDtypeStruct((2, VREGS, 8, 128), f32),
            jax.ShapeDtypeStruct((4,), i32),
            jax.ShapeDtypeStruct((2, 9, VREGS, 8, 128), i32),
            jax.ShapeDtypeStruct((2, 2, VREGS, 8, 128), i32),
        ],
        in_specs=[vmem] * 4,
        out_specs=[vmem, vmem, vmem, smem, vmem, vmem],
        scratch_shapes=[pltpu.VMEM((VREGS, 8, 128), i32), pltpu.VMEM((256, 128), f32)],
        compiler_params=pltpu.CompilerParams(vmem_limit_bytes=32 << 20),
        cost_estimate=pl.CostEstimate(flops=20_000_000, bytes_accessed=8_000_000, transcendentals=0),
        name="plan",
    )(cells.reshape(256, 128), offsets.reshape(2, 256, 128), moves.reshape(256, 128), slots.reshape(256, 128))


def pack_kernel(ocean, mass, momentum, out):
    lane = lax.broadcasted_iota(i32, (8, 128), 1)
    tiles = LON * BLOCKS

    def tile(part, k):
        k = k % tiles
        return ocean[part, :, 128 * k : 128 * k + 128]

    spots = (0, 1, 4, 5)
    for b in range(LON):
        rim = jnp.zeros((8, 128), f32)
        for part in range(4):
            for k in range(BLOCKS):
                column = (part * BLOCKS + k) * 128
                out[b, :, column : column + 128] = tile(part, BLOCKS * b + k)
            spot = spots[part]
            rim = jnp.where(lane == spot, pltpu.roll(tile(part, BLOCKS * b - 1), spot + 1, 1), rim)
            rim = jnp.where(lane == spot + 2, pltpu.roll(tile(part, BLOCKS * b + BLOCKS), spot + 2, 1), rim)
        out[b, :, 4 * COLS : 4 * COLS + 128] = rim
    lanes = lax.broadcasted_iota(i32, (ROWS, 128), 1)
    beside = jnp.ones((ROWS, 128), f32)
    for side in range(2):
        column = 0 if side else COLS - 128
        sources = [mass[:, column : column + 128]] * 2 + [
            momentum[part, :, column : column + 128] for part in range(2)
        ]
        for source, spot in zip(sources, spots):
            spot = spot + 2 * side
            shift = spot if side else spot + 1
            beside = jnp.where(lanes == spot, pltpu.roll(source, shift, 1), beside)
    turned = jnp.transpose(beside)[0:8]
    for b in range(LON):
        out[b, :, 4 * COLS + 128 : 4 * COLS + 256] = turned


def pack(ocean, mass, momentum):
    vmem = pl.BlockSpec(memory_space=pltpu.VMEM)
    return pl.pallas_call(
        pack_kernel,
        out_shape=jax.ShapeDtypeStruct((LON, 8, 4 * COLS + 256), f32),
        in_specs=[vmem] * 3,
        out_specs=vmem,
        name="pack",
    )(ocean, mass, momentum)


def drive(momentum, stress, mass, current):
    return (momentum + step_dt * stress + step_dt * drag_coef * mass * current) / (
        mass * (1.0 + step_dt * drag_coef)
    )


def table_kernel(beside_spots, forcing, mass, momentum, table, first_edge, last_edge):
    lane = lax.broadcasted_iota(i32, (ROWS, 128), 1)
    rim = forcing[:, :, 4 * COLS : 4 * COLS + 128].reshape(ROWS, 128)
    west = forcing[beside_spots[0], :, 4 * COLS + 128 : 4 * COLS + 256]
    east = forcing[beside_spots[1], :, 4 * COLS + 128 : 4 * COLS + 256]
    beside = jnp.where((sublane_ids() & 2) == 0, west, east)
    beside = jnp.concatenate([beside] + [jnp.ones((120, 128), f32)], axis=0)
    beside = jnp.transpose(beside)
    rim = drive(pltpu.roll(beside, 124, 1), pltpu.roll(rim, 124, 1), beside, rim)
    for part in range(2):
        blocks, after, before = [], [], []
        for k in range(BLOCKS):
            column = 128 * k
            current = forcing[:, :, COLS * part + column : COLS * part + column + 128]
            stress = forcing[:, :, COLS * (2 + part) + column : COLS * (2 + part) + column + 128]
            block = drive(
                momentum[part, :, column : column + 128],
                stress.reshape(ROWS, 128),
                mass[:, column : column + 128],
                current.reshape(ROWS, 128),
            )
            blocks.append(block)
            after.append(pltpu.roll(block, 1, 1))
            before.append(pltpu.roll(block, 127, 1))
        left = [pltpu.roll(rim, 127, 1) if part else rim] + after[:-1]
        right = before[1:] + [pltpu.roll(rim, 125 - part, 1)]
        for k in range(BLOCKS):
            shifted = (
                jnp.where(lane == 0, left[k], after[k]),
                blocks[k],
                jnp.where(lane == 127, right[k], before[k]),
            )
            for q in range(3):
                plane = part * 3 + q
                for r in range(0, ROWS, 8):
                    table[pl.ds((ROWS * k + r) * 8 + plane, 8, stride=8), :] = shifted[q][r : r + 8]
    for plane in (6, 7):
        for r in range(0, PLANE, 8):
            table[pl.ds(r * 8 + plane, 8, stride=8), :] = jnp.zeros((8, 128), f32)
    for k in range(BLOCKS):
        top, end = ROWS * k * 8, (ROWS * k + ROWS - 1) * 8
        first_edge[8 * k : 8 * k + 8, :] = table[top : top + 8, :]
        last_edge[8 * k : 8 * k + 8, :] = table[end : end + 8, :]


def node_table(beside_spots, forcing, mass, momentum):
    vmem = pl.BlockSpec(memory_space=pltpu.VMEM)
    return pl.pallas_call(
        table_kernel,
        out_shape=[
            jax.ShapeDtypeStruct((8 * PLANE, 128), f32),
            jax.ShapeDtypeStruct((24, 128), f32),
            jax.ShapeDtypeStruct((24, 128), f32),
        ],
        in_specs=[pl.BlockSpec(memory_space=pltpu.SMEM)] + [vmem] * 3,
        out_specs=[vmem] * 3,
        name="table",
    )(beside_spots, forcing, mass, momentum)


def spline(frac):
    lower = 0.5 * (0.5 - frac) * (0.5 - frac)
    middle = 0.75 - frac * frac
    upper = 0.5 * (0.5 + frac) * (0.5 + frac)
    return (lower, middle, upper)


def interpolate_group(g, ends, near, frac, nodes, address, samples, state):
    half = lax.shift_right_logical(g, 4)
    low = (g & 15) * 8
    start = (g & 3) * 64 + lax.shift_right_logical(g, 2)
    first = [ends[half, low + j] for j in range(8)]
    last = [ends[half + 2, low + j] for j in range(8)]
    span = last[0] - first[0]
    for j in range(1, 8):
        span = jnp.maximum(span, last[j] - first[j])

    def trip(step, sums):
        sums = list(sums)
        for j in range(8):
            spot = near[pl.ds(start + 8 * j, 8, stride=0), :]
            lanes = spot & 127
            chunk = lax.shift_right_logical(spot, 7)
            for more in range(2):
                here = jnp.minimum(first[j] + 2 * step + more, last[j])
                base = address(here)
                inside = chunk == here
                for r in range(3):
                    tile = nodes[pl.ds(pl.multiple_of((base + r - 1) * 8, 8), 8), :]
                    sums[3 * j + r] = jnp.where(inside, from_lanes(tile, lanes), sums[3 * j + r])
        return tuple(sums)

    trips = lax.shift_right_logical(span, 1) + 1
    sums = lax.fori_loop(0, trips, trip, tuple(jnp.zeros((8, 128), f32) for _ in range(24)))
    for j in range(8):
        for r in range(3):
            samples[pl.ds(r * 64 + j, 8, stride=8), :] = sums[3 * j + r]
    rows = pl.ds(start, 8, stride=8)
    d_row = frac[0, rows, :]
    d_col = frac[1, rows, :]
    w_row = spline(d_row)
    w_col = spline(d_col)
    arm_row = [4.0 * w_row[r] * (r - 1 - d_row) for r in range(3)]
    arm_col = [4.0 * w_col[q] * (q - 1 - d_col) for q in range(3)]
    speeds = []
    affines = []
    for part in range(2):
        speed = along_row = along_col = None
        for q in range(3):
            plane = part * 3 + q
            got = [samples[r * 64 + plane * 8 : r * 64 + plane * 8 + 8, :] for r in range(3)]
            plain = w_row[0] * got[0] + w_row[1] * got[1] + w_row[2] * got[2]
            tilted = arm_row[0] * got[0] + arm_row[1] * got[1] + arm_row[2] * got[2]
            terms = (w_col[q] * plain, w_col[q] * tilted, arm_col[q] * plain)
            if q == 0:
                speed, along_row, along_col = terms
            else:
                speed = speed + terms[0]
                along_row = along_row + terms[1]
                along_col = along_col + terms[2]
        speeds.append(speed)
        affines += [along_row, along_col]
    values = [d_row + step_dt * speeds[0], d_col + step_dt * speeds[1]] + speeds + affines
    for c in range(8):
        state[c, rows, :] = values[c]


def group_first(g, ends):
    return ends[lax.shift_right_logical(g, 4), (g & 15) * 8]


def inner_kernel(ends, table, near, frac, state, samples):
    def group(g, carry):
        @pl.when(group_first(g, ends) >= 8)
        def _():
            interpolate_group(
                g, ends, near, frac, table, lambda chunk: chunk - 8, samples, state
            )

        return carry

    lax.fori_loop(0, VREGS, group, 0)


def inner(ends, table, near, frac):
    vmem = pl.BlockSpec(memory_space=pltpu.VMEM)
    smem = pl.BlockSpec(memory_space=pltpu.SMEM)
    return pl.pallas_call(
        inner_kernel,
        out_shape=jax.ShapeDtypeStruct((8, 256, 128), f32),
        in_specs=[smem] + [vmem] * 3,
        out_specs=vmem,
        scratch_shapes=[pltpu.VMEM((192, 128), f32)],
        compiler_params=pltpu.CompilerParams(vmem_limit_bytes=24 << 20),
        cost_estimate=pl.CostEstimate(flops=20_000_000, bytes_accessed=8_000_000, transcendentals=0),
        name="inner",
    )(ends, table, near.reshape(256, 128), frac.reshape(2, 256, 128))


def transfer_kernel(
    ends, counts,
    table, above, below, near, frac, early, index, words,
    state, north, south, east, west,
    nodes, samples, columns, buffer,
):
    for c in range(8):
        state[c] = early[c]
    nodes[0 : 8 * PLANE, :] = table[...]

    def fill(spot, tile):
        nodes[(PLANE + spot) * 8 : (PLANE + spot) * 8 + 8, :] = tile

    for k in range(BLOCKS):
        top, end = ROWS * k * 8, (ROWS * k + ROWS - 1) * 8
        fill(8 * k, above[8 * k : 8 * k + 8, :])
        fill(8 * k + 1, table[top : top + 8, :])
        fill(8 * k + 2, table[top + 8 : top + 16, :])
        fill(8 * k + 4, table[end - 8 : end, :])
        fill(8 * k + 5, table[end : end + 8, :])
        fill(8 * k + 6, below[8 * k : 8 * k + 8, :])

    def address(chunk):
        return jnp.where(chunk < 8, PLANE + 1 + 4 * chunk, jnp.maximum(chunk - 8, 1))

    def group(g, carry):
        @pl.when(group_first(g, ends) < 8)
        def _():
            interpolate_group(g, ends, near, frac, nodes, address, samples, state)

        return carry

    lax.fori_loop(0, VREGS, group, 0)

    direction = lax.shift_right_logical(sublane_ids(), 1)
    count = jnp.where(
        direction < 2,
        jnp.where(direction == 0, counts[0], counts[1]),
        jnp.where(direction == 2, counts[2], counts[3]),
    )
    slot = (sublane_ids() & 1) * 4096 + lane_ids()

    def finish(v, moved):
        kept = slot + v * 128 < count
        for c in range(8):
            columns[pl.ds(v * 8 + c, 8, stride=256), :] = jnp.where(kept, moved[c], 0.0)

    apply_network(
        8,
        lambda c, v: state[c, 8 * v : 8 * v + 8, :],
        buffer, index.at[0], words.at[0, 0], words.at[0, 1], finish,
    )
    for k, out in enumerate((north, south, east, west)):
        for j in range(64):
            base = (k * 64 + j) * 8
            out[:, 128 * j : 128 * j + 128] = columns[base : base + 8, :]


def transfer(ends, counts, table, above, below, near, frac, early, index, words):
    vmem = pl.BlockSpec(memory_space=pltpu.VMEM)
    smem = pl.BlockSpec(memory_space=pltpu.SMEM)
    return pl.pallas_call(
        transfer_kernel,
        out_shape=[jax.ShapeDtypeStruct((8, 256, 128), f32)]
        + [jax.ShapeDtypeStruct((8, CAP), f32)] * 4,
        in_specs=[smem] * 2 + [vmem] * 8,
        out_specs=[vmem] * 5,
        scratch_shapes=[
            pltpu.VMEM((8 * EDGE_PLANE, 128), f32),
            pltpu.VMEM((192, 128), f32),
            pltpu.VMEM((2048, 128), f32),
            pltpu.VMEM((8, VREGS, 8, 128), f32),
        ],
        compiler_params=pltpu.CompilerParams(vmem_limit_bytes=32 << 20),
        cost_estimate=pl.CostEstimate(flops=10_000_000, bytes_accessed=8_000_000, transcendentals=0),
        name="transfer",
    )(
        ends, counts, table, above, below,
        near.reshape(256, 128), frac.reshape(2, 256, 128), early, index, words,
    )


def restore_kernel(state, offsets, index, words, out, columns, buffer):
    def finish(v, moved):
        for c in range(2):
            frac = offsets[c, pl.ds(v, 8, stride=32), :]
            columns[pl.ds(v * 8 + c, 8, stride=256), :] = frac + step_dt * moved[c]
        for c in range(6):
            columns[pl.ds(v * 8 + c + 2, 8, stride=256), :] = moved[c]

    apply_network(
        6,
        lambda c, v: state[c + 2, 8 * v : 8 * v + 8, :],
        buffer, index.at[1], words.at[1, 0], words.at[1, 1], finish,
    )
    for j in range(256):
        out[:, 128 * j : 128 * j + 128] = columns[8 * j : 8 * j + 8, :]


def restore(state, offsets, index, words):
    vmem = pl.BlockSpec(memory_space=pltpu.VMEM)
    return pl.pallas_call(
        restore_kernel,
        out_shape=jax.ShapeDtypeStruct((8, 4 * CAP), f32),
        in_specs=[vmem] * 4,
        out_specs=vmem,
        scratch_shapes=[pltpu.VMEM((2048, 128), f32), pltpu.VMEM((6, VREGS, 8, 128), f32)],
        compiler_params=pltpu.CompilerParams(vmem_limit_bytes=32 << 20),
        cost_estimate=pl.CostEstimate(flops=10_000_000, bytes_accessed=4_000_000, transcendentals=0),
        name="restore",
    )(state, offsets.reshape(2, 256, 128), index, words)


def from_behind(block, axis, distance):
    devices = range(lax.axis_size(axis))
    route = [(i - distance, i) for i in devices if i - distance in devices]
    return lax.ppermute(block, axis, route)


def passed_along(value, axis, by):
    count = lax.axis_size(axis)
    return lax.ppermute(value, axis, [(i, (i + by) % count) for i in range(count)])


def shards(ocean, grid_mass, grid_momentum, cells, offsets, moves, slots):
    outgoing = pack(ocean, grid_mass, grid_momentum)
    forcing = lax.all_to_all(outgoing, "lon", 0, 0)
    near, ends, frac, counts, index, words = plan(cells, offsets, moves, slots)
    forcing, near = lax.optimization_barrier((forcing, near))
    here = lax.axis_index("lon")
    beside_spots = jnp.stack([(here + LON - 1) % LON, (here + 1) % LON])
    table, first_edge, last_edge = node_table(beside_spots, forcing, grid_mass, grid_momentum)
    above = from_behind(last_edge, "lat", 1)
    below = from_behind(first_edge, "lat", -1)
    early = inner(ends, table, near, frac)
    state, north, south, east, west = transfer(
        ends, counts, table, above, below, near, frac, early, index, words
    )
    north = from_behind(north, "lat", 1)
    south = from_behind(south, "lat", -1)
    east = passed_along(east, "lon", 1)
    west = passed_along(west, "lon", -1)
    parcels = restore(state, offsets, index, words)
    return (parcels, jnp.concatenate([north, south, east, west], axis=1))


def solution(mesh):
    in_specs = (
        P(None, ("lat", "lon"), None),
        P("lat", "lon"),
        P(None, "lat", "lon"),
        P(("lat", "lon")),
        P(None, ("lat", "lon")),
        P(("lat", "lon")),
        P(("lat", "lon")),
    )
    out_specs = (P(None, ("lat", "lon")), P(None, ("lat", "lon")))
    return jax.shard_map(shards, mesh=mesh, in_specs=in_specs, out_specs=out_specs, check_vma=False)
```

```python
import jax
import jax.numpy as jnp
from jax import lax
from jax.experimental import pallas as pl
from jax.experimental.pallas import tpu as pltpu
from jax.sharding import PartitionSpec as P

CAP = 8192
ROWS = 128
COLS = 384
BLOCKS = 3
VREGS = 32
PLANE = BLOCKS * ROWS
EDGE_PLANE = PLANE + 32
LON = 16

step_dt = 0.5
drag_coef = 2.0

f32 = jnp.float32
i32 = jnp.int32


def lane_ids():
    return lax.broadcasted_iota(i32, (8, 128), 1)


def sublane_ids():
    return lax.broadcasted_iota(i32, (8, 128), 0)


def from_lanes(x, index):
    return jnp.take_along_axis(x, index, axis=1, mode="promise_in_bounds")


def from_sublanes(x, index):
    return jnp.take_along_axis(x, index, axis=0, mode="promise_in_bounds")


def bit_set(words, place):
    return lax.shift_left(words, 31 - place) < 0


def lane_pass(xs, distance_bit, uppers, perm):
    out = []
    for v, x in enumerate(xs):
        other = from_lanes(x, perm)
        out.append(
            jnp.where(uppers[v % len(uppers)], jnp.maximum(x, other), jnp.minimum(x, other))
        )
    return out


def lane_bit(k):
    return lax.shift_right_logical(lane_ids(), k) & 1


def lane_passes(xs, top, flips):
    lane = lane_ids()
    for j in range(top, -1, -1):
        uppers = [(lane_bit(j) ^ flip) != 0 for flip in flips]
        xs = lane_pass(xs, j, uppers, lane ^ (1 << j))
    return xs


def sort_network(keys, payloads, record):
    lane = lane_ids()
    lane_f = lane.astype(f32)
    sub = sublane_ids()
    words = [jnp.zeros((8, 128), i32) for _ in range(VREGS)] if record else None
    sub_words = [jnp.zeros((8, 128), i32) for _ in range(VREGS)] if record else None

    xs = [key * 128.0 + lane_f for key in keys]
    for k in range(1, 7):
        xs = lane_passes(xs, k - 1, (lane_bit(k),))
    xs = lane_passes(xs, 6, (0, 1))

    def settle(t, xs):
        out = []
        for v in range(VREGS):
            index = xs[v].astype(i32) & 127
            if record:
                record(t, v, index)
            for payload in payloads:
                payload[v] = from_lanes(payload[v], index)
            out.append(xs[v] - index.astype(f32) + lane_f)
        return out

    xs = settle(0, xs)
    for t in range(1, 9):
        sign = None
        if 5 <= t <= 7:
            sign = jnp.where((lax.shift_right_logical(sub, t - 5) & 1) != 0, -1.0, 1.0)
            xs = [x * sign for x in xs]
        for i in range(t - 1, -1, -1):
            if i >= 5:
                near = i - 5
                perm = sub ^ (1 << near)
                upper = (lax.shift_right_logical(sub, near) & 1) != 0
                for v in range(VREGS):
                    x = xs[v]
                    other = from_sublanes(x, perm)
                    take = jnp.where(upper, other, x) > jnp.where(upper, x, other)
                    xs[v] = jnp.where(take, other, x)
                    if record:
                        sub_words[v] = sub_words[v] | jnp.where(take, 1 << sub_place(t, i), 0)
                    for payload in payloads:
                        y = payload[v]
                        payload[v] = jnp.where(take, from_sublanes(y, perm), y)
            else:
                for a in range(VREGS):
                    if a & (1 << i):
                        continue
                    b = a | (1 << i)
                    x, y = xs[a], xs[b]
                    down = t <= 4 and (a >> t) & 1
                    swap = x < y if down else x > y
                    low, high = jnp.minimum(x, y), jnp.maximum(x, y)
                    xs[a], xs[b] = (high, low) if down else (low, high)
                    if record:
                        words[a] = words[a] | jnp.where(swap, 1 << row_place(t, i), 0)
                    for payload in payloads:
                        x, y = payload[a], payload[b]
                        payload[a] = jnp.where(swap, y, x)
                        payload[b] = jnp.where(swap, x, y)
        if t == 8 and not record:
            break
        if t <= 4:
            runs = [xs[v] for v in range(VREGS)]
            lane_done = []
            ups = [v for v in range(VREGS) if not (v >> t) & 1]
            downs = [v for v in range(VREGS) if (v >> t) & 1]
            up_x = lane_passes([runs[v] for v in ups], 6, (0,))
            down_x = lane_passes([runs[v] for v in downs], 6, (1,)) if downs else []
            for v, x in zip(ups, up_x):
                xs[v] = x
            for v, x in zip(downs, down_x):
                xs[v] = x
        else:
            xs = lane_passes(xs, 6, (0,))
            if sign is not None:
                xs = [x * sign for x in xs]
        xs = settle(t, xs)
    return xs, words, sub_words


def row_place(t, i):
    return t * (t - 1) // 2 + t - 1 - i if t <= 5 else 5 * t - 15 + 4 - i


def sub_place(t, i):
    return {6: 0, 7: 1, 8: 3}[t] + t - 1 - i


def apply_network(count, source, buffer, index, words, sub_words, finish):
    sub = sublane_ids()
    def lane_phase(t, v, get):
        lanes = index[t, v]
        moved = [from_lanes(get(c), lanes) for c in range(count)]
        for i in range(t, 4, -1):
            if t < 8:
                take = bit_set(sub_words[v], sub_place(t + 1, i))
                perm = sub ^ (1 << (i - 5))
                moved = [jnp.where(take, from_sublanes(x, perm), x) for x in moved]
        return moved

    for v in range(VREGS):
        for c, x in enumerate(lane_phase(0, v, lambda c: source(c, v))):
            buffer[c, v] = x
    for t in range(1, 9):
        top = min(t, 5)
        rounds = {1: ((0,),), 2: ((1, 0),), 3: ((2, 1, 0),), 4: ((3, 2), (1, 0)), 5: ((4, 3), (2, 1, 0))}[top]
        for bits in rounds:
            mask = sum(1 << i for i in bits)
            for base in range(VREGS):
                if base & mask:
                    continue
                members = [v for v in range(VREGS) if v & ~mask == base]
                swaps = {}
                for i in bits:
                    for a in members:
                        if not a & (1 << i):
                            swaps[i, a] = bit_set(words[a], row_place(t, i))
                for c in range(count):
                    xs = {v: buffer[c, v] for v in members}
                    for i in bits:
                        for a in members:
                            if a & (1 << i):
                                continue
                            b = a | (1 << i)
                            x, y = xs[a], xs[b]
                            xs[a] = jnp.where(swaps[i, a], y, x)
                            xs[b] = jnp.where(swaps[i, a], x, y)
                    for v in members:
                        buffer[c, v] = xs[v]
        for v in range(VREGS):
            moved = lane_phase(t, v, lambda c: buffer[c, v])
            if t < 8:
                for c in range(count):
                    buffer[c, v] = moved[c]
            else:
                finish(v, moved)


def plan_kernel(
    cells, offsets, moves, slots,
    near_out, ends_out, frac_out, counts_out,
    index_out, words_out,
    tags, chunks,
):
    lane = lane_ids()
    sub = sublane_ids()
    stay = jnp.where(moves[...] == 0, 1.0, 0.0)
    before = jnp.where(
        lax.broadcasted_iota(i32, (128, 128), 0) < lax.broadcasted_iota(i32, (128, 128), 1), 1.0, 0.0
    )
    rank = jnp.dot(stay, before, preferred_element_type=f32)
    above = jnp.where(
        lax.broadcasted_iota(i32, (256, 256), 1) < lax.broadcasted_iota(i32, (256, 256), 0), 1.0, 0.0
    )
    totals = jnp.broadcast_to(jnp.sum(stay, axis=1, keepdims=True), (256, 128))
    rank = rank + jnp.dot(above, totals, preferred_element_type=f32)
    rank = rank.astype(i32)
    counts = []
    for k in range(4):
        count = jnp.sum(jnp.where(moves[...] == k + 1, 1.0, 0.0)).astype(i32)
        counts.append(count)
        counts_out[k] = count
    hole = rank + counts[0]
    filled = counts[0]
    for k in range(1, 4):
        hole = hole + jnp.where(rank >= k * CAP - filled, counts[k], 0)
        filled = filled + counts[k]
    target = jnp.where(moves[...] > 0, (moves[...] - 1) * CAP + slots[...], hole)
    number = lax.broadcasted_iota(i32, (256, 128), 0) * 128 + lax.broadcasted_iota(i32, (256, 128), 1)
    cell = cells[...]
    row = (cell.astype(f32) * (1.0 / COLS)).astype(i32)
    row = row - jnp.where(row * COLS > cell, 1, 0)
    row = row + jnp.where((row + 1) * COLS <= cell, 1, 0)
    col = cell - row * COLS
    part = lax.shift_right_logical(col, 7)
    edge = jnp.where(row == 0, 0, 1)
    inner = (row > 0) & (row < ROWS - 1)
    spot = jnp.where(inner, 8 + part * ROWS + row, 2 * part + edge) * 128 + (col & 127)
    keys = []
    for v in range(VREGS):
        part = slice(v * 8, v * 8 + 8)
        keys.append(spot[part].astype(f32))
        tags[v] = lax.shift_left(target[part], 15) | number[part]
        frac_out[0, v] = offsets[0, part]
        frac_out[1, v] = offsets[1, part]
    keys, _, _ = sort_network(keys, (frac_out.at[0], frac_out.at[1], tags), None)
    for v in range(VREGS):
        spots = lax.shift_right_logical(keys[v].astype(i32), 7)
        near_out[v] = spots
        chunks[pl.ds(v, 8, stride=32), :] = lax.shift_right_logical(spots, 7).astype(f32)
    for half in range(2):
        turned = jnp.transpose(chunks[half * 128 : half * 128 + 128, :])
        ends_out[half : half + 1, :] = jnp.min(turned, axis=0, keepdims=True).astype(i32)
        ends_out[half + 2 : half + 3, :] = jnp.max(turned, axis=0, keepdims=True).astype(i32)

    def one(which, carry):
        keys = [
            (lax.shift_right_logical(tags[v], jnp.where(which == 0, 15, 0)) & 32767).astype(f32)
            for v in range(VREGS)
        ]

        def record(t, v, index):
            index_out[which, t, v] = index

        _, words, sub_words = sort_network(keys, (), record)
        for v in range(VREGS):
            words_out[which, 0, v] = words[v]
            words_out[which, 1, v] = sub_words[v]
        return carry

    lax.fori_loop(0, 2, one, 0)


def plan(cells, offsets, moves, slots):
    vmem = pl.BlockSpec(memory_space=pltpu.VMEM)
    smem = pl.BlockSpec(memory_space=pltpu.SMEM)
    return pl.pallas_call(
        plan_kernel,
        out_shape=[
            jax.ShapeDtypeStruct((VREGS, 8, 128), i32),
            jax.ShapeDtypeStruct((4, 128), i32),
            jax.ShapeDtypeStruct((2, VREGS, 8, 128), f32),
            jax.ShapeDtypeStruct((4,), i32),
            jax.ShapeDtypeStruct((2, 9, VREGS, 8, 128), i32),
            jax.ShapeDtypeStruct((2, 2, VREGS, 8, 128), i32),
        ],
        in_specs=[vmem] * 4,
        out_specs=[vmem, vmem, vmem, smem, vmem, vmem],
        scratch_shapes=[pltpu.VMEM((VREGS, 8, 128), i32), pltpu.VMEM((256, 128), f32)],
        compiler_params=pltpu.CompilerParams(vmem_limit_bytes=32 << 20),
        cost_estimate=pl.CostEstimate(flops=20_000_000, bytes_accessed=8_000_000, transcendentals=0),
        name="plan",
    )(cells.reshape(256, 128), offsets.reshape(2, 256, 128), moves.reshape(256, 128), slots.reshape(256, 128))


def pack_kernel(ocean, mass, momentum, out):
    lane = lax.broadcasted_iota(i32, (8, 128), 1)
    tiles = LON * BLOCKS

    def tile(part, k):
        k = k % tiles
        return ocean[part, :, 128 * k : 128 * k + 128]

    spots = (0, 1, 4, 5)
    for b in range(LON):
        rim = jnp.zeros((8, 128), f32)
        for part in range(4):
            for k in range(BLOCKS):
                column = (part * BLOCKS + k) * 128
                out[b, :, column : column + 128] = tile(part, BLOCKS * b + k)
            spot = spots[part]
            rim = jnp.where(lane == spot, pltpu.roll(tile(part, BLOCKS * b - 1), spot + 1, 1), rim)
            rim = jnp.where(lane == spot + 2, pltpu.roll(tile(part, BLOCKS * b + BLOCKS), spot + 2, 1), rim)
        out[b, :, 4 * COLS : 4 * COLS + 128] = rim
    lanes = lax.broadcasted_iota(i32, (ROWS, 128), 1)
    beside = jnp.ones((ROWS, 128), f32)
    for side in range(2):
        column = 0 if side else COLS - 128
        sources = [mass[:, column : column + 128]] * 2 + [
            momentum[part, :, column : column + 128] for part in range(2)
        ]
        for source, spot in zip(sources, spots):
            spot = spot + 2 * side
            shift = spot if side else spot + 1
            beside = jnp.where(lanes == spot, pltpu.roll(source, shift, 1), beside)
    turned = jnp.transpose(beside)[0:8]
    for b in range(LON):
        out[b, :, 4 * COLS + 128 : 4 * COLS + 256] = turned


def pack(ocean, mass, momentum):
    vmem = pl.BlockSpec(memory_space=pltpu.VMEM)
    return pl.pallas_call(
        pack_kernel,
        out_shape=jax.ShapeDtypeStruct((LON, 8, 4 * COLS + 256), f32),
        in_specs=[vmem] * 3,
        out_specs=vmem,
        name="pack",
    )(ocean, mass, momentum)


def drive(momentum, stress, mass, current):
    return (momentum + step_dt * stress + step_dt * drag_coef * mass * current) / (
        mass * (1.0 + step_dt * drag_coef)
    )


def table_kernel(forcing, mass, momentum, table, first_edge, last_edge):
    lane = lax.broadcasted_iota(i32, (ROWS, 128), 1)
    rim = forcing[:, :, 4 * COLS : 4 * COLS + 128].reshape(ROWS, 128)
    here = lax.axis_index("lon")
    west = forcing[lax.rem(here + LON - 1, LON), :, 4 * COLS + 128 : 4 * COLS + 256]
    east = forcing[lax.rem(here + 1, LON), :, 4 * COLS + 128 : 4 * COLS + 256]
    beside = jnp.where((sublane_ids() & 2) == 0, west, east)
    beside = jnp.concatenate([beside] + [jnp.ones((120, 128), f32)], axis=0)
    beside = jnp.transpose(beside)
    rim = drive(pltpu.roll(beside, 124, 1), pltpu.roll(rim, 124, 1), beside, rim)
    for part in range(2):
        blocks, after, before = [], [], []
        for k in range(BLOCKS):
            column = 128 * k
            current = forcing[:, :, COLS * part + column : COLS * part + column + 128]
            stress = forcing[:, :, COLS * (2 + part) + column : COLS * (2 + part) + column + 128]
            block = drive(
                momentum[part, :, column : column + 128],
                stress.reshape(ROWS, 128),
                mass[:, column : column + 128],
                current.reshape(ROWS, 128),
            )
            blocks.append(block)
            after.append(pltpu.roll(block, 1, 1))
            before.append(pltpu.roll(block, 127, 1))
        left = [pltpu.roll(rim, 127, 1) if part else rim] + after[:-1]
        right = before[1:] + [pltpu.roll(rim, 125 - part, 1)]
        for k in range(BLOCKS):
            shifted = (
                jnp.where(lane == 0, left[k], after[k]),
                blocks[k],
                jnp.where(lane == 127, right[k], before[k]),
            )
            for q in range(3):
                plane = part * 3 + q
                for r in range(0, ROWS, 8):
                    table[pl.ds((ROWS * k + r) * 8 + plane, 8, stride=8), :] = shifted[q][r : r + 8]
    for plane in (6, 7):
        for r in range(0, PLANE, 8):
            table[pl.ds(r * 8 + plane, 8, stride=8), :] = jnp.zeros((8, 128), f32)
    for k in range(BLOCKS):
        top, end = ROWS * k * 8, (ROWS * k + ROWS - 1) * 8
        first_edge[8 * k : 8 * k + 8, :] = table[top : top + 8, :]
        last_edge[8 * k : 8 * k + 8, :] = table[end : end + 8, :]


def node_table(forcing, mass, momentum):
    vmem = pl.BlockSpec(memory_space=pltpu.VMEM)
    return pl.pallas_call(
        table_kernel,
        out_shape=[
            jax.ShapeDtypeStruct((8 * PLANE, 128), f32),
            jax.ShapeDtypeStruct((24, 128), f32),
            jax.ShapeDtypeStruct((24, 128), f32),
        ],
        in_specs=[vmem] * 3,
        out_specs=[vmem] * 3,
        name="table",
    )(forcing, mass, momentum)


def spline(frac):
    lower = 0.5 * (0.5 - frac) * (0.5 - frac)
    middle = 0.75 - frac * frac
    upper = 0.5 * (0.5 + frac) * (0.5 + frac)
    return (lower, middle, upper)


def interpolate_group(g, ends, near, frac, nodes, address, samples, state):
    half = lax.shift_right_logical(g, 4)
    low = (g & 15) * 8
    start = (g & 3) * 64 + lax.shift_right_logical(g, 2)
    first = [ends[half, low + j] for j in range(8)]
    last = [ends[half + 2, low + j] for j in range(8)]
    span = last[0] - first[0]
    for j in range(1, 8):
        span = jnp.maximum(span, last[j] - first[j])

    def trip(step, sums):
        sums = list(sums)
        for j in range(8):
            spot = near[pl.ds(start + 8 * j, 8, stride=0), :]
            lanes = spot & 127
            chunk = lax.shift_right_logical(spot, 7)
            for more in range(3):
                here = jnp.minimum(first[j] + 3 * step + more, last[j])
                base = address(here)
                inside = chunk == here
                for r in range(3):
                    tile = nodes[pl.ds(pl.multiple_of((base + r - 1) * 8, 8), 8), :]
                    sums[3 * j + r] = jnp.where(inside, from_lanes(tile, lanes), sums[3 * j + r])
        return tuple(sums)

    trips = lax.shift_right_logical(span * 171, 9) + 1
    sums = trip(0, tuple(jnp.zeros((8, 128), f32) for _ in range(24)))
    sums = lax.fori_loop(1, trips, trip, sums)
    for j in range(8):
        for r in range(3):
            samples[pl.ds(r * 64 + j, 8, stride=8), :] = sums[3 * j + r]
    rows = pl.ds(start, 8, stride=8)
    d_row = frac[0, rows, :]
    d_col = frac[1, rows, :]
    w_row = spline(d_row)
    w_col = spline(d_col)
    arm_row = [4.0 * w_row[r] * (r - 1 - d_row) for r in range(3)]
    arm_col = [4.0 * w_col[q] * (q - 1 - d_col) for q in range(3)]
    speeds = []
    affines = []
    for part in range(2):
        speed = along_row = along_col = None
        for q in range(3):
            plane = part * 3 + q
            got = [samples[r * 64 + plane * 8 : r * 64 + plane * 8 + 8, :] for r in range(3)]
            plain = w_row[0] * got[0] + w_row[1] * got[1] + w_row[2] * got[2]
            tilted = arm_row[0] * got[0] + arm_row[1] * got[1] + arm_row[2] * got[2]
            terms = (w_col[q] * plain, w_col[q] * tilted, arm_col[q] * plain)
            if q == 0:
                speed, along_row, along_col = terms
            else:
                speed = speed + terms[0]
                along_row = along_row + terms[1]
                along_col = along_col + terms[2]
        speeds.append(speed)
        affines += [along_row, along_col]
    values = [d_row + step_dt * speeds[0], d_col + step_dt * speeds[1]] + speeds + affines
    for c in range(8):
        state[c, rows, :] = values[c]


def group_first(g, ends):
    return ends[lax.shift_right_logical(g, 4), (g & 15) * 8]


def inner_kernel(ends, table, near, frac, state, samples):
    def group(g, carry):
        @pl.when(group_first(g, ends) >= 8)
        def _():
            interpolate_group(
                g, ends, near, frac, table, lambda chunk: chunk - 8, samples, state
            )

        return carry

    lax.fori_loop(0, VREGS, group, 0)


def inner(ends, table, near, frac):
    vmem = pl.BlockSpec(memory_space=pltpu.VMEM)
    smem = pl.BlockSpec(memory_space=pltpu.SMEM)
    return pl.pallas_call(
        inner_kernel,
        out_shape=jax.ShapeDtypeStruct((8, 256, 128), f32),
        in_specs=[smem] + [vmem] * 3,
        out_specs=vmem,
        scratch_shapes=[pltpu.VMEM((192, 128), f32)],
        compiler_params=pltpu.CompilerParams(vmem_limit_bytes=24 << 20),
        cost_estimate=pl.CostEstimate(flops=20_000_000, bytes_accessed=8_000_000, transcendentals=0),
        name="inner",
    )(ends, table, near.reshape(256, 128), frac.reshape(2, 256, 128))


def transfer_kernel(
    ends, counts,
    table, above, below, near, frac, early, index, words,
    state, north, south, east, west,
    nodes, samples, columns, buffer,
):
    for c in range(8):
        state[c] = early[c]
    nodes[0 : 8 * PLANE, :] = table[...]

    def fill(spot, tile):
        nodes[(PLANE + spot) * 8 : (PLANE + spot) * 8 + 8, :] = tile

    for k in range(BLOCKS):
        top, end = ROWS * k * 8, (ROWS * k + ROWS - 1) * 8
        fill(8 * k, above[8 * k : 8 * k + 8, :])
        fill(8 * k + 1, table[top : top + 8, :])
        fill(8 * k + 2, table[top + 8 : top + 16, :])
        fill(8 * k + 4, table[end - 8 : end, :])
        fill(8 * k + 5, table[end : end + 8, :])
        fill(8 * k + 6, below[8 * k : 8 * k + 8, :])

    def address(chunk):
        return jnp.where(chunk < 8, PLANE + 1 + 4 * chunk, jnp.maximum(chunk - 8, 1))

    def group(g, carry):
        @pl.when(group_first(g, ends) < 8)
        def _():
            interpolate_group(g, ends, near, frac, nodes, address, samples, state)

        return carry

    lax.fori_loop(0, VREGS, group, 0)

    direction = lax.shift_right_logical(sublane_ids(), 1)
    count = jnp.where(
        direction < 2,
        jnp.where(direction == 0, counts[0], counts[1]),
        jnp.where(direction == 2, counts[2], counts[3]),
    )
    slot = (sublane_ids() & 1) * 4096 + lane_ids()

    def finish(v, moved):
        kept = slot + v * 128 < count
        for c in range(8):
            columns[pl.ds(v * 8 + c, 8, stride=256), :] = jnp.where(kept, moved[c], 0.0)

    apply_network(
        8,
        lambda c, v: state[c, 8 * v : 8 * v + 8, :],
        buffer, index.at[0], words.at[0, 0], words.at[0, 1], finish,
    )
    for k, out in enumerate((north, south, east, west)):
        for j in range(64):
            base = (k * 64 + j) * 8
            out[:, 128 * j : 128 * j + 128] = columns[base : base + 8, :]


def transfer(ends, counts, table, above, below, near, frac, early, index, words):
    vmem = pl.BlockSpec(memory_space=pltpu.VMEM)
    smem = pl.BlockSpec(memory_space=pltpu.SMEM)
    return pl.pallas_call(
        transfer_kernel,
        out_shape=[jax.ShapeDtypeStruct((8, 256, 128), f32)]
        + [jax.ShapeDtypeStruct((8, CAP), f32)] * 4,
        in_specs=[smem] * 2 + [vmem] * 8,
        out_specs=[vmem] * 5,
        scratch_shapes=[
            pltpu.VMEM((8 * EDGE_PLANE, 128), f32),
            pltpu.VMEM((192, 128), f32),
            pltpu.VMEM((2048, 128), f32),
            pltpu.VMEM((8, VREGS, 8, 128), f32),
        ],
        compiler_params=pltpu.CompilerParams(vmem_limit_bytes=32 << 20),
        cost_estimate=pl.CostEstimate(flops=10_000_000, bytes_accessed=8_000_000, transcendentals=0),
        name="transfer",
    )(
        ends, counts, table, above, below,
        near.reshape(256, 128), frac.reshape(2, 256, 128), early, index, words,
    )


def restore_kernel(state, offsets, index, words, out, columns, buffer):
    def finish(v, moved):
        for c in range(2):
            frac = offsets[c, pl.ds(v, 8, stride=32), :]
            columns[pl.ds(v * 8 + c, 8, stride=256), :] = frac + step_dt * moved[c]
        for c in range(6):
            columns[pl.ds(v * 8 + c + 2, 8, stride=256), :] = moved[c]

    apply_network(
        6,
        lambda c, v: state[c + 2, 8 * v : 8 * v + 8, :],
        buffer, index.at[1], words.at[1, 0], words.at[1, 1], finish,
    )
    for j in range(256):
        out[:, 128 * j : 128 * j + 128] = columns[8 * j : 8 * j + 8, :]


def restore(state, offsets, index, words):
    vmem = pl.BlockSpec(memory_space=pltpu.VMEM)
    return pl.pallas_call(
        restore_kernel,
        out_shape=jax.ShapeDtypeStruct((8, 4 * CAP), f32),
        in_specs=[vmem] * 4,
        out_specs=vmem,
        scratch_shapes=[pltpu.VMEM((2048, 128), f32), pltpu.VMEM((6, VREGS, 8, 128), f32)],
        compiler_params=pltpu.CompilerParams(vmem_limit_bytes=32 << 20),
        cost_estimate=pl.CostEstimate(flops=10_000_000, bytes_accessed=4_000_000, transcendentals=0),
        name="restore",
    )(state, offsets.reshape(2, 256, 128), index, words)


def from_behind(block, axis, distance):
    devices = range(lax.axis_size(axis))
    route = [(i - distance, i) for i in devices if i - distance in devices]
    return lax.ppermute(block, axis, route)


def passed_along(value, axis, by):
    count = lax.axis_size(axis)
    return lax.ppermute(value, axis, [(i, (i + by) % count) for i in range(count)])


def shards(ocean, grid_mass, grid_momentum, cells, offsets, moves, slots):
    outgoing = pack(ocean, grid_mass, grid_momentum)
    forcing = lax.all_to_all(outgoing, "lon", 0, 0)
    near, ends, frac, counts, index, words = plan(cells, offsets, moves, slots)
    forcing, near = lax.optimization_barrier((forcing, near))
    table, first_edge, last_edge = node_table(forcing, grid_mass, grid_momentum)
    above = from_behind(last_edge, "lat", 1)
    below = from_behind(first_edge, "lat", -1)
    early = inner(ends, table, near, frac)
    state, north, south, east, west = transfer(
        ends, counts, table, above, below, near, frac, early, index, words
    )
    north = from_behind(north, "lat", 1)
    south = from_behind(south, "lat", -1)
    east = passed_along(east, "lon", 1)
    west = passed_along(west, "lon", -1)
    parcels = restore(state, offsets, index, words)
    return (parcels, jnp.concatenate([north, south, east, west], axis=1))


def solution(mesh):
    in_specs = (
        P(None, ("lat", "lon"), None),
        P("lat", "lon"),
        P(None, "lat", "lon"),
        P(("lat", "lon")),
        P(None, ("lat", "lon")),
        P(("lat", "lon")),
        P(("lat", "lon")),
    )
    out_specs = (P(None, ("lat", "lon")), P(None, ("lat", "lon")))
    return jax.shard_map(shards, mesh=mesh, in_specs=in_specs, out_specs=out_specs, check_vma=False)
```

```python
import jax
import jax.numpy as jnp
from jax import lax
from jax.experimental import pallas as pl
from jax.experimental.pallas import tpu as pltpu
from jax.sharding import PartitionSpec as P

CAP = 8192
ROWS = 128
COLS = 384
BLOCKS = 3
VREGS = 32
PLANE = BLOCKS * ROWS
EDGE_PLANE = PLANE + 32
LON = 16

step_dt = 0.5
drag_coef = 2.0

f32 = jnp.float32
i32 = jnp.int32


def lane_ids():
    return lax.broadcasted_iota(i32, (8, 128), 1)


def sublane_ids():
    return lax.broadcasted_iota(i32, (8, 128), 0)


def from_lanes(x, index):
    return jnp.take_along_axis(x, index, axis=1, mode="promise_in_bounds")


def from_sublanes(x, index):
    return jnp.take_along_axis(x, index, axis=0, mode="promise_in_bounds")


def bit_set(words, place):
    return lax.shift_left(words, 31 - place) < 0


def lane_pass(xs, distance_bit, uppers, perm):
    out = []
    for v, x in enumerate(xs):
        other = from_lanes(x, perm)
        out.append(
            jnp.where(uppers[v % len(uppers)], jnp.maximum(x, other), jnp.minimum(x, other))
        )
    return out


def lane_bit(k):
    return lax.shift_right_logical(lane_ids(), k) & 1


def lane_passes(xs, top, flips):
    lane = lane_ids()
    for j in range(top, -1, -1):
        uppers = [(lane_bit(j) ^ flip) != 0 for flip in flips]
        xs = lane_pass(xs, j, uppers, lane ^ (1 << j))
    return xs


def sort_network(keys, payloads, record):
    lane = lane_ids()
    lane_f = lane.astype(f32)
    sub = sublane_ids()
    words = [jnp.zeros((8, 128), i32) for _ in range(VREGS)] if record else None
    sub_words = [jnp.zeros((8, 128), i32) for _ in range(VREGS)] if record else None

    xs = [key * 128.0 + lane_f for key in keys]
    for k in range(1, 7):
        xs = lane_passes(xs, k - 1, (lane_bit(k),))
    xs = lane_passes(xs, 6, (0, 1))

    def settle(t, xs):
        out = []
        for v in range(VREGS):
            index = xs[v].astype(i32) & 127
            if record:
                record(t, v, index)
            for payload in payloads:
                payload[v] = from_lanes(payload[v], index)
            out.append(xs[v] - index.astype(f32) + lane_f)
        return out

    xs = settle(0, xs)
    for t in range(1, 9):
        sign = None
        if 5 <= t <= 7:
            sign = jnp.where((lax.shift_right_logical(sub, t - 5) & 1) != 0, -1.0, 1.0)
            xs = [x * sign for x in xs]
        for i in range(t - 1, -1, -1):
            if i >= 5:
                near = i - 5
                perm = sub ^ (1 << near)
                upper = (lax.shift_right_logical(sub, near) & 1) != 0
                for v in range(VREGS):
                    x = xs[v]
                    other = from_sublanes(x, perm)
                    take = jnp.where(upper, other, x) > jnp.where(upper, x, other)
                    xs[v] = jnp.where(take, other, x)
                    if record:
                        sub_words[v] = sub_words[v] | jnp.where(take, 1 << sub_place(t, i), 0)
                    for payload in payloads:
                        y = payload[v]
                        payload[v] = jnp.where(take, from_sublanes(y, perm), y)
            else:
                for a in range(VREGS):
                    if a & (1 << i):
                        continue
                    b = a | (1 << i)
                    x, y = xs[a], xs[b]
                    down = t <= 4 and (a >> t) & 1
                    swap = x < y if down else x > y
                    low, high = jnp.minimum(x, y), jnp.maximum(x, y)
                    xs[a], xs[b] = (high, low) if down else (low, high)
                    if record:
                        words[a] = words[a] | jnp.where(swap, 1 << row_place(t, i), 0)
                    for payload in payloads:
                        x, y = payload[a], payload[b]
                        payload[a] = jnp.where(swap, y, x)
                        payload[b] = jnp.where(swap, x, y)
        if t == 8 and not record:
            break
        if t <= 4:
            runs = [xs[v] for v in range(VREGS)]
            lane_done = []
            ups = [v for v in range(VREGS) if not (v >> t) & 1]
            downs = [v for v in range(VREGS) if (v >> t) & 1]
            up_x = lane_passes([runs[v] for v in ups], 6, (0,))
            down_x = lane_passes([runs[v] for v in downs], 6, (1,)) if downs else []
            for v, x in zip(ups, up_x):
                xs[v] = x
            for v, x in zip(downs, down_x):
                xs[v] = x
        else:
            xs = lane_passes(xs, 6, (0,))
            if sign is not None:
                xs = [x * sign for x in xs]
        xs = settle(t, xs)
    return xs, words, sub_words


def row_place(t, i):
    return t * (t - 1) // 2 + t - 1 - i if t <= 5 else 5 * t - 15 + 4 - i


def sub_place(t, i):
    return {6: 0, 7: 1, 8: 3}[t] + t - 1 - i


def apply_network(count, source, buffer, index, words, sub_words, finish):
    sub = sublane_ids()
    def lane_phase(t, v, get):
        lanes = index[t, v]
        moved = [from_lanes(get(c), lanes) for c in range(count)]
        for i in range(t, 4, -1):
            if t < 8:
                take = bit_set(sub_words[v], sub_place(t + 1, i))
                perm = sub ^ (1 << (i - 5))
                moved = [jnp.where(take, from_sublanes(x, perm), x) for x in moved]
        return moved

    for v in range(VREGS):
        for c, x in enumerate(lane_phase(0, v, lambda c: source(c, v))):
            buffer[c, v] = x
    for t in range(1, 9):
        top = min(t, 5)
        rounds = {1: ((0,),), 2: ((1, 0),), 3: ((2, 1, 0),), 4: ((3, 2), (1, 0)), 5: ((4, 3), (2, 1, 0))}[top]
        for bits in rounds:
            mask = sum(1 << i for i in bits)
            for base in range(VREGS):
                if base & mask:
                    continue
                members = [v for v in range(VREGS) if v & ~mask == base]
                swaps = {}
                for i in bits:
                    for a in members:
                        if not a & (1 << i):
                            swaps[i, a] = bit_set(words[a], row_place(t, i))
                for c in range(count):
                    xs = {v: buffer[c, v] for v in members}
                    for i in bits:
                        for a in members:
                            if a & (1 << i):
                                continue
                            b = a | (1 << i)
                            x, y = xs[a], xs[b]
                            xs[a] = jnp.where(swaps[i, a], y, x)
                            xs[b] = jnp.where(swaps[i, a], x, y)
                    for v in members:
                        buffer[c, v] = xs[v]
        for v in range(VREGS):
            moved = lane_phase(t, v, lambda c: buffer[c, v])
            if t < 8:
                for c in range(count):
                    buffer[c, v] = moved[c]
            else:
                finish(v, moved)


def plan_kernel(
    packed, offsets,
    near_out, ends_out, frac_out, counts_out,
    index_out, words_out, tags,
    moves, chunks,
):
    lane = lane_ids()
    sub = sublane_ids()
    moves[...] = lax.shift_right_logical(packed[...], 29)
    slots = lax.shift_right_logical(packed[...], 16) & (CAP - 1)
    stay = jnp.where(moves[...] == 0, 1.0, 0.0)
    before = jnp.where(
        lax.broadcasted_iota(i32, (128, 128), 0) < lax.broadcasted_iota(i32, (128, 128), 1), 1.0, 0.0
    )
    rank = jnp.dot(stay, before, preferred_element_type=f32)
    above = jnp.where(
        lax.broadcasted_iota(i32, (256, 256), 1) < lax.broadcasted_iota(i32, (256, 256), 0), 1.0, 0.0
    )
    totals = jnp.broadcast_to(jnp.sum(stay, axis=1, keepdims=True), (256, 128))
    rank = rank + jnp.dot(above, totals, preferred_element_type=f32)
    rank = rank.astype(i32)
    counts = []
    for k in range(4):
        count = jnp.sum(jnp.where(moves[...] == k + 1, 1.0, 0.0)).astype(i32)
        counts.append(count)
        counts_out[k] = count
    hole = rank + counts[0]
    filled = counts[0]
    for k in range(1, 4):
        hole = hole + jnp.where(rank >= k * CAP - filled, counts[k], 0)
        filled = filled + counts[k]
    target = jnp.where(moves[...] > 0, (moves[...] - 1) * CAP + slots, hole)
    number = lax.broadcasted_iota(i32, (256, 128), 0) * 128 + lax.broadcasted_iota(i32, (256, 128), 1)
    cell = packed[...] & 65535
    row = (cell.astype(f32) * (1.0 / COLS)).astype(i32)
    row = row - jnp.where(row * COLS > cell, 1, 0)
    row = row + jnp.where((row + 1) * COLS <= cell, 1, 0)
    col = cell - row * COLS
    part = lax.shift_right_logical(col, 7)
    edge = jnp.where(row == 0, 0, 1)
    inner = (row > 0) & (row < ROWS - 1)
    spot = jnp.where(inner, 8 + part * ROWS + row, 2 * part + edge) * 128 + (col & 127)
    keys = []
    for v in range(VREGS):
        part = slice(v * 8, v * 8 + 8)
        keys.append(spot[part].astype(f32))
        tags[v] = lax.shift_left(target[part], 15) | number[part]
        frac_out[0, v] = offsets[0, part]
        frac_out[1, v] = offsets[1, part]
    keys, _, _ = sort_network(keys, (frac_out.at[0], frac_out.at[1], tags), None)
    for v in range(VREGS):
        spots = lax.shift_right_logical(keys[v].astype(i32), 7)
        near_out[v] = spots
        chunks[pl.ds(v, 8, stride=32), :] = lax.shift_right_logical(spots, 7).astype(f32)
    for half in range(2):
        turned = jnp.transpose(chunks[half * 128 : half * 128 + 128, :])
        ends_out[half : half + 1, :] = jnp.min(turned, axis=0, keepdims=True).astype(i32)
        ends_out[half + 2 : half + 3, :] = jnp.max(turned, axis=0, keepdims=True).astype(i32)

    plan_moves(lambda v: lax.shift_right_logical(tags[v], 15), index_out, words_out)


def plan_moves(rank, index_out, words_out):
    keys = [rank(v).astype(f32) for v in range(VREGS)]

    def record(t, v, index):
        index_out[t, v] = index

    _, words, sub_words = sort_network(keys, (), record)
    for v in range(VREGS):
        words_out[0, v] = words[v]
        words_out[1, v] = sub_words[v]


def plan(cells, offsets, moves, slots):
    packed = cells | lax.shift_left(slots, 16) | lax.shift_left(moves, 29)
    vmem = pl.BlockSpec(memory_space=pltpu.VMEM)
    smem = pl.BlockSpec(memory_space=pltpu.SMEM)
    return pl.pallas_call(
        plan_kernel,
        out_shape=[
            jax.ShapeDtypeStruct((VREGS, 8, 128), i32),
            jax.ShapeDtypeStruct((4, 128), i32),
            jax.ShapeDtypeStruct((2, VREGS, 8, 128), f32),
            jax.ShapeDtypeStruct((4,), i32),
            jax.ShapeDtypeStruct((9, VREGS, 8, 128), i32),
            jax.ShapeDtypeStruct((2, VREGS, 8, 128), i32),
            jax.ShapeDtypeStruct((VREGS, 8, 128), i32),
        ],
        in_specs=[vmem] * 2,
        out_specs=[vmem, vmem, vmem, smem, vmem, vmem, vmem],
        scratch_shapes=[pltpu.VMEM((256, 128), i32), pltpu.VMEM((256, 128), f32)],
        compiler_params=pltpu.CompilerParams(vmem_limit_bytes=32 << 20),
        cost_estimate=pl.CostEstimate(flops=20_000_000, bytes_accessed=8_000_000, transcendentals=0),
        name="plan",
    )(packed.reshape(256, 128), offsets.reshape(2, 256, 128))


def pack_kernel(ocean, mass, momentum, out):
    lane = lax.broadcasted_iota(i32, (8, 128), 1)
    tiles = LON * BLOCKS

    def tile(part, k):
        k = k % tiles
        return ocean[part, :, 128 * k : 128 * k + 128]

    spots = (0, 1, 4, 5)
    for b in range(LON):
        rim = jnp.zeros((8, 128), f32)
        for part in range(4):
            for k in range(BLOCKS):
                column = (part * BLOCKS + k) * 128
                out[b, :, column : column + 128] = tile(part, BLOCKS * b + k)
            spot = spots[part]
            rim = jnp.where(lane == spot, pltpu.roll(tile(part, BLOCKS * b - 1), spot + 1, 1), rim)
            rim = jnp.where(lane == spot + 2, pltpu.roll(tile(part, BLOCKS * b + BLOCKS), spot + 2, 1), rim)
        out[b, :, 4 * COLS : 4 * COLS + 128] = rim
    lanes = lax.broadcasted_iota(i32, (ROWS, 128), 1)
    beside = jnp.ones((ROWS, 128), f32)
    for side in range(2):
        column = 0 if side else COLS - 128
        sources = [mass[:, column : column + 128]] * 2 + [
            momentum[part, :, column : column + 128] for part in range(2)
        ]
        for source, spot in zip(sources, spots):
            spot = spot + 2 * side
            shift = spot if side else spot + 1
            beside = jnp.where(lanes == spot, pltpu.roll(source, shift, 1), beside)
    turned = jnp.transpose(beside)[0:8]
    for b in range(LON):
        out[b, :, 4 * COLS + 128 : 4 * COLS + 256] = turned


def pack(ocean, mass, momentum):
    vmem = pl.BlockSpec(memory_space=pltpu.VMEM)
    return pl.pallas_call(
        pack_kernel,
        out_shape=jax.ShapeDtypeStruct((LON, 8, 4 * COLS + 256), f32),
        in_specs=[vmem] * 3,
        out_specs=vmem,
        name="pack",
    )(ocean, mass, momentum)


def drive(momentum, stress, mass, current):
    return (momentum + step_dt * stress + step_dt * drag_coef * mass * current) / (
        mass * (1.0 + step_dt * drag_coef)
    )


def table_kernel(forcing, mass, momentum, table, first_edge, last_edge):
    lane = lax.broadcasted_iota(i32, (ROWS, 128), 1)
    rim = forcing[:, :, 4 * COLS : 4 * COLS + 128].reshape(ROWS, 128)
    here = lax.axis_index("lon")
    west = forcing[lax.rem(here + LON - 1, LON), :, 4 * COLS + 128 : 4 * COLS + 256]
    east = forcing[lax.rem(here + 1, LON), :, 4 * COLS + 128 : 4 * COLS + 256]
    beside = jnp.where((sublane_ids() & 2) == 0, west, east)
    beside = jnp.concatenate([beside] + [jnp.ones((120, 128), f32)], axis=0)
    beside = jnp.transpose(beside)
    rim = drive(pltpu.roll(beside, 124, 1), pltpu.roll(rim, 124, 1), beside, rim)
    for part in range(2):
        blocks, after, before = [], [], []
        for k in range(BLOCKS):
            column = 128 * k
            current = forcing[:, :, COLS * part + column : COLS * part + column + 128]
            stress = forcing[:, :, COLS * (2 + part) + column : COLS * (2 + part) + column + 128]
            block = drive(
                momentum[part, :, column : column + 128],
                stress.reshape(ROWS, 128),
                mass[:, column : column + 128],
                current.reshape(ROWS, 128),
            )
            blocks.append(block)
            after.append(pltpu.roll(block, 1, 1))
            before.append(pltpu.roll(block, 127, 1))
        left = [pltpu.roll(rim, 127, 1) if part else rim] + after[:-1]
        right = before[1:] + [pltpu.roll(rim, 125 - part, 1)]
        for k in range(BLOCKS):
            shifted = (
                jnp.where(lane == 0, left[k], after[k]),
                blocks[k],
                jnp.where(lane == 127, right[k], before[k]),
            )
            for q in range(3):
                plane = part * 3 + q
                for r in range(0, ROWS, 8):
                    table[pl.ds((ROWS * k + r) * 8 + plane, 8, stride=8), :] = shifted[q][r : r + 8]
    for plane in (6, 7):
        for r in range(0, PLANE, 8):
            table[pl.ds(r * 8 + plane, 8, stride=8), :] = jnp.zeros((8, 128), f32)
    for k in range(BLOCKS):
        top, end = ROWS * k * 8, (ROWS * k + ROWS - 1) * 8
        first_edge[8 * k : 8 * k + 8, :] = table[top : top + 8, :]
        last_edge[8 * k : 8 * k + 8, :] = table[end : end + 8, :]


def node_table(forcing, mass, momentum):
    vmem = pl.BlockSpec(memory_space=pltpu.VMEM)
    return pl.pallas_call(
        table_kernel,
        out_shape=[
            jax.ShapeDtypeStruct((8 * PLANE, 128), f32),
            jax.ShapeDtypeStruct((24, 128), f32),
            jax.ShapeDtypeStruct((24, 128), f32),
        ],
        in_specs=[vmem] * 3,
        out_specs=[vmem] * 3,
        compiler_params=pltpu.CompilerParams(vmem_limit_bytes=40 << 20),
        name="table",
    )(forcing, mass, momentum)


def spline(frac):
    lower = 0.5 * (0.5 - frac) * (0.5 - frac)
    middle = 0.75 - frac * frac
    upper = 0.5 * (0.5 + frac) * (0.5 + frac)
    return (lower, middle, upper)


def interpolate_group(g, ends, near, frac, nodes, address, samples, state):
    half = lax.shift_right_logical(g, 4)
    low = (g & 15) * 8
    start = (g & 3) * 64 + lax.shift_right_logical(g, 2)
    first = [ends[half, low + j] for j in range(8)]
    last = [ends[half + 2, low + j] for j in range(8)]
    span = last[0] - first[0]
    for j in range(1, 8):
        span = jnp.maximum(span, last[j] - first[j])

    def trip(step, sums):
        sums = list(sums)
        for j in range(8):
            spot = near[pl.ds(start + 8 * j, 8, stride=0), :]
            lanes = spot & 127
            chunk = lax.shift_right_logical(spot, 7)
            for more in range(3):
                here = jnp.minimum(first[j] + 3 * step + more, last[j])
                base = address(here)
                inside = chunk == here
                for r in range(3):
                    tile = nodes[pl.ds(pl.multiple_of((base + r - 1) * 8, 8), 8), :]
                    sums[3 * j + r] = jnp.where(inside, from_lanes(tile, lanes), sums[3 * j + r])
        return tuple(sums)

    trips = lax.shift_right_logical(span * 171, 9) + 1
    sums = trip(0, tuple(jnp.zeros((8, 128), f32) for _ in range(24)))
    sums = lax.fori_loop(1, trips, trip, sums)
    for j in range(8):
        for r in range(3):
            samples[pl.ds(r * 64 + j, 8, stride=8), :] = sums[3 * j + r]
    rows = pl.ds(start, 8, stride=8)
    d_row = frac[0, rows, :]
    d_col = frac[1, rows, :]
    w_row = spline(d_row)
    w_col = spline(d_col)
    arm_row = [4.0 * w_row[r] * (r - 1 - d_row) for r in range(3)]
    arm_col = [4.0 * w_col[q] * (q - 1 - d_col) for q in range(3)]
    speeds = []
    affines = []
    for part in range(2):
        speed = along_row = along_col = None
        for q in range(3):
            plane = part * 3 + q
            got = [samples[r * 64 + plane * 8 : r * 64 + plane * 8 + 8, :] for r in range(3)]
            plain = w_row[0] * got[0] + w_row[1] * got[1] + w_row[2] * got[2]
            tilted = arm_row[0] * got[0] + arm_row[1] * got[1] + arm_row[2] * got[2]
            terms = (w_col[q] * plain, w_col[q] * tilted, arm_col[q] * plain)
            if q == 0:
                speed, along_row, along_col = terms
            else:
                speed = speed + terms[0]
                along_row = along_row + terms[1]
                along_col = along_col + terms[2]
        speeds.append(speed)
        affines += [along_row, along_col]
    values = [d_row + step_dt * speeds[0], d_col + step_dt * speeds[1]] + speeds + affines
    for c in range(8):
        state[c, rows, :] = values[c]


def group_first(g, ends):
    return ends[lax.shift_right_logical(g, 4), (g & 15) * 8]


def inner_kernel(ends, table, near, frac, state, samples):
    def group(g, carry):
        @pl.when(group_first(g, ends) >= 8)
        def _():
            interpolate_group(
                g, ends, near, frac, table, lambda chunk: chunk - 8, samples, state
            )

        return carry

    lax.fori_loop(0, VREGS, group, 0)


def inner(ends, table, near, frac):
    vmem = pl.BlockSpec(memory_space=pltpu.VMEM)
    smem = pl.BlockSpec(memory_space=pltpu.SMEM)
    return pl.pallas_call(
        inner_kernel,
        out_shape=jax.ShapeDtypeStruct((8, 256, 128), f32),
        in_specs=[smem] + [vmem] * 3,
        out_specs=vmem,
        scratch_shapes=[pltpu.VMEM((192, 128), f32)],
        compiler_params=pltpu.CompilerParams(vmem_limit_bytes=24 << 20),
        cost_estimate=pl.CostEstimate(flops=20_000_000, bytes_accessed=8_000_000, transcendentals=0),
        name="inner",
    )(ends, table, near.reshape(256, 128), frac.reshape(2, 256, 128))


def transfer_kernel(
    ends, counts,
    table, above, below, near, frac, early, index, words,
    state, north, south, east, west,
    nodes, samples, columns, buffer,
):
    for c in range(8):
        state[c] = early[c]
    nodes[0 : 8 * PLANE, :] = table[...]

    def fill(spot, tile):
        nodes[(PLANE + spot) * 8 : (PLANE + spot) * 8 + 8, :] = tile

    for k in range(BLOCKS):
        top, end = ROWS * k * 8, (ROWS * k + ROWS - 1) * 8
        fill(8 * k, above[8 * k : 8 * k + 8, :])
        fill(8 * k + 1, table[top : top + 8, :])
        fill(8 * k + 2, table[top + 8 : top + 16, :])
        fill(8 * k + 4, table[end - 8 : end, :])
        fill(8 * k + 5, table[end : end + 8, :])
        fill(8 * k + 6, below[8 * k : 8 * k + 8, :])

    def address(chunk):
        return jnp.where(chunk < 8, PLANE + 1 + 4 * chunk, jnp.maximum(chunk - 8, 1))

    def group(g, carry):
        @pl.when(group_first(g, ends) < 8)
        def _():
            interpolate_group(g, ends, near, frac, nodes, address, samples, state)

        return carry

    lax.fori_loop(0, VREGS, group, 0)

    direction = lax.shift_right_logical(sublane_ids(), 1)
    count = jnp.where(
        direction < 2,
        jnp.where(direction == 0, counts[0], counts[1]),
        jnp.where(direction == 2, counts[2], counts[3]),
    )
    slot = (sublane_ids() & 1) * 4096 + lane_ids()

    def finish(v, moved):
        kept = slot + v * 128 < count
        for c in range(8):
            columns[pl.ds(v * 8 + c, 8, stride=256), :] = jnp.where(kept, moved[c], 0.0)

    apply_network(
        8,
        lambda c, v: state[c, 8 * v : 8 * v + 8, :],
        buffer, index, words.at[0], words.at[1], finish,
    )
    for k, out in enumerate((north, south, east, west)):
        for j in range(64):
            base = (k * 64 + j) * 8
            out[:, 128 * j : 128 * j + 128] = columns[base : base + 8, :]


def transfer(ends, counts, table, above, below, near, frac, early, index, words):
    vmem = pl.BlockSpec(memory_space=pltpu.VMEM)
    smem = pl.BlockSpec(memory_space=pltpu.SMEM)
    return pl.pallas_call(
        transfer_kernel,
        out_shape=[jax.ShapeDtypeStruct((8, 256, 128), f32)]
        + [jax.ShapeDtypeStruct((8, CAP), f32)] * 4,
        in_specs=[smem] * 2 + [vmem] * 8,
        out_specs=[vmem] * 5,
        scratch_shapes=[
            pltpu.VMEM((8 * EDGE_PLANE, 128), f32),
            pltpu.VMEM((192, 128), f32),
            pltpu.VMEM((2048, 128), f32),
            pltpu.VMEM((8, VREGS, 8, 128), f32),
        ],
        compiler_params=pltpu.CompilerParams(vmem_limit_bytes=32 << 20),
        cost_estimate=pl.CostEstimate(flops=10_000_000, bytes_accessed=8_000_000, transcendentals=0),
        name="transfer",
    )(
        ends, counts, table, above, below,
        near.reshape(256, 128), frac.reshape(2, 256, 128), early, index, words,
    )


def restore_kernel(state, offsets, tags, out, columns, buffer, index, words):
    plan_moves(lambda v: tags[v] & 32767, index, words)

    def finish(v, moved):
        for c in range(2):
            frac = offsets[c, pl.ds(v, 8, stride=32), :]
            columns[pl.ds(v * 8 + c, 8, stride=256), :] = frac + step_dt * moved[c]
        for c in range(6):
            columns[pl.ds(v * 8 + c + 2, 8, stride=256), :] = moved[c]

    apply_network(
        6,
        lambda c, v: state[c + 2, 8 * v : 8 * v + 8, :],
        buffer, index, words.at[0], words.at[1], finish,
    )
    for j in range(256):
        out[:, 128 * j : 128 * j + 128] = columns[8 * j : 8 * j + 8, :]


def restore(state, offsets, tags):
    vmem = pl.BlockSpec(memory_space=pltpu.VMEM)
    return pl.pallas_call(
        restore_kernel,
        out_shape=jax.ShapeDtypeStruct((8, 4 * CAP), f32),
        in_specs=[vmem] * 3,
        out_specs=vmem,
        scratch_shapes=[
            pltpu.VMEM((2048, 128), f32),
            pltpu.VMEM((6, VREGS, 8, 128), f32),
            pltpu.VMEM((9, VREGS, 8, 128), i32),
            pltpu.VMEM((2, VREGS, 8, 128), i32),
        ],
        compiler_params=pltpu.CompilerParams(vmem_limit_bytes=32 << 20),
        cost_estimate=pl.CostEstimate(flops=10_000_000, bytes_accessed=4_000_000, transcendentals=0),
        name="restore",
    )(state, offsets.reshape(2, 256, 128), tags)


def from_behind(block, axis, distance):
    devices = range(lax.axis_size(axis))
    route = [(i - distance, i) for i in devices if i - distance in devices]
    return lax.ppermute(block, axis, route)


def passed_along(value, axis, by):
    count = lax.axis_size(axis)
    return lax.ppermute(value, axis, [(i, (i + by) % count) for i in range(count)])


def shards(ocean, grid_mass, grid_momentum, cells, offsets, moves, slots):
    outgoing = pack(ocean, grid_mass, grid_momentum)
    forcing = lax.all_to_all(outgoing, "lon", 0, 0)
    near, ends, frac, counts, index, words, tags = plan(cells, offsets, moves, slots)
    forcing, near = lax.optimization_barrier((forcing, near))
    table, first_edge, last_edge = node_table(forcing, grid_mass, grid_momentum)
    above = from_behind(last_edge, "lat", 1)
    below = from_behind(first_edge, "lat", -1)
    early = inner(ends, table, near, frac)
    state, north, south, east, west = transfer(
        ends, counts, table, above, below, near, frac, early, index, words
    )
    north = from_behind(north, "lat", 1)
    south = from_behind(south, "lat", -1)
    east = passed_along(east, "lon", 1)
    west = passed_along(west, "lon", -1)
    parcels = restore(state, offsets, tags)
    return (parcels, jnp.concatenate([north, south, east, west], axis=1))


def solution(mesh):
    in_specs = (
        P(None, ("lat", "lon"), None),
        P("lat", "lon"),
        P(None, "lat", "lon"),
        P(("lat", "lon")),
        P(None, ("lat", "lon")),
        P(("lat", "lon")),
        P(("lat", "lon")),
    )
    out_specs = (P(None, ("lat", "lon")), P(None, ("lat", "lon")))
    return jax.shard_map(shards, mesh=mesh, in_specs=in_specs, out_specs=out_specs, check_vma=False)
```

```python
import jax
import jax.numpy as jnp
from jax import lax
from jax.experimental import pallas as pl
from jax.experimental.pallas import tpu as pltpu
from jax.sharding import PartitionSpec as P

CAP = 8192
ROWS = 128
COLS = 384
BLOCKS = 3
VREGS = 32
PLANE = BLOCKS * ROWS
EDGE_PLANE = PLANE + 32
LON = 16

step_dt = 0.5
drag_coef = 2.0

f32 = jnp.float32
i32 = jnp.int32


def lane_ids():
    return lax.broadcasted_iota(i32, (8, 128), 1)


def sublane_ids():
    return lax.broadcasted_iota(i32, (8, 128), 0)


def from_lanes(x, index):
    return jnp.take_along_axis(x, index, axis=1, mode="promise_in_bounds")


def from_sublanes(x, index):
    return jnp.take_along_axis(x, index, axis=0, mode="promise_in_bounds")


def bit_set(words, place):
    return lax.shift_left(words, 31 - place) < 0


def lane_pass(xs, distance_bit, uppers, perm):
    out = []
    for v, x in enumerate(xs):
        other = from_lanes(x, perm)
        out.append(
            jnp.where(uppers[v % len(uppers)], jnp.maximum(x, other), jnp.minimum(x, other))
        )
    return out


def lane_bit(k):
    return lax.shift_right_logical(lane_ids(), k) & 1


def lane_passes(xs, top, flips):
    lane = lane_ids()
    for j in range(top, -1, -1):
        uppers = [(lane_bit(j) ^ flip) != 0 for flip in flips]
        xs = lane_pass(xs, j, uppers, lane ^ (1 << j))
    return xs


def sort_network(keys, payloads, record):
    lane = lane_ids()
    lane_f = lane.astype(f32)
    sub = sublane_ids()
    words = [jnp.zeros((8, 128), i32) for _ in range(VREGS)] if record else None
    sub_words = [jnp.zeros((8, 128), i32) for _ in range(VREGS)] if record else None

    xs = [key * 128.0 + lane_f for key in keys]
    for k in range(1, 7):
        xs = lane_passes(xs, k - 1, (lane_bit(k),))
    xs = lane_passes(xs, 6, (0, 1))

    def settle(t, xs):
        out = []
        for v in range(VREGS):
            index = xs[v].astype(i32) & 127
            if record:
                record(t, v, index)
            for payload in payloads:
                payload[v] = from_lanes(payload[v], index)
            out.append(xs[v] - index.astype(f32) + lane_f)
        return out

    xs = settle(0, xs)
    for t in range(1, 9):
        sign = None
        if 5 <= t <= 7:
            sign = jnp.where((lax.shift_right_logical(sub, t - 5) & 1) != 0, -1.0, 1.0)
            xs = [x * sign for x in xs]
        for i in range(t - 1, -1, -1):
            if i >= 5:
                near = i - 5
                perm = sub ^ (1 << near)
                upper = (lax.shift_right_logical(sub, near) & 1) != 0
                for v in range(VREGS):
                    x = xs[v]
                    other = from_sublanes(x, perm)
                    take = jnp.where(upper, other, x) > jnp.where(upper, x, other)
                    xs[v] = jnp.where(take, other, x)
                    if record:
                        sub_words[v] = sub_words[v] | jnp.where(take, 1 << sub_place(t, i), 0)
                    for payload in payloads:
                        y = payload[v]
                        payload[v] = jnp.where(take, from_sublanes(y, perm), y)
            else:
                for a in range(VREGS):
                    if a & (1 << i):
                        continue
                    b = a | (1 << i)
                    x, y = xs[a], xs[b]
                    down = t <= 4 and (a >> t) & 1
                    swap = x < y if down else x > y
                    low, high = jnp.minimum(x, y), jnp.maximum(x, y)
                    xs[a], xs[b] = (high, low) if down else (low, high)
                    if record:
                        words[a] = words[a] | jnp.where(swap, 1 << row_place(t, i), 0)
                    for payload in payloads:
                        x, y = payload[a], payload[b]
                        payload[a] = jnp.where(swap, y, x)
                        payload[b] = jnp.where(swap, x, y)
        if t == 8 and not record:
            break
        if t <= 4:
            runs = [xs[v] for v in range(VREGS)]
            lane_done = []
            ups = [v for v in range(VREGS) if not (v >> t) & 1]
            downs = [v for v in range(VREGS) if (v >> t) & 1]
            up_x = lane_passes([runs[v] for v in ups], 6, (0,))
            down_x = lane_passes([runs[v] for v in downs], 6, (1,)) if downs else []
            for v, x in zip(ups, up_x):
                xs[v] = x
            for v, x in zip(downs, down_x):
                xs[v] = x
        else:
            xs = lane_passes(xs, 6, (0,))
            if sign is not None:
                xs = [x * sign for x in xs]
        xs = settle(t, xs)
    return xs, words, sub_words


def row_place(t, i):
    return t * (t - 1) // 2 + t - 1 - i if t <= 5 else 5 * t - 15 + 4 - i


def sub_place(t, i):
    return {6: 0, 7: 1, 8: 3}[t] + t - 1 - i


def apply_network(count, source, buffer, index, words, sub_words, finish):
    sub = sublane_ids()
    def lane_phase(t, v, get):
        lanes = index[t, v]
        moved = [from_lanes(get(c), lanes) for c in range(count)]
        for i in range(t, 4, -1):
            if t < 8:
                take = bit_set(sub_words[v], sub_place(t + 1, i))
                perm = sub ^ (1 << (i - 5))
                moved = [jnp.where(take, from_sublanes(x, perm), x) for x in moved]
        return moved

    for v in range(VREGS):
        for c, x in enumerate(lane_phase(0, v, lambda c: source(c, v))):
            buffer[c, v] = x
    for t in range(1, 9):
        top = min(t, 5)
        rounds = {1: ((0,),), 2: ((1, 0),), 3: ((2, 1, 0),), 4: ((3, 2), (1, 0)), 5: ((4, 3), (2, 1, 0))}[top]
        for bits in rounds:
            mask = sum(1 << i for i in bits)
            for base in range(VREGS):
                if base & mask:
                    continue
                members = [v for v in range(VREGS) if v & ~mask == base]
                swaps = {}
                for i in bits:
                    for a in members:
                        if not a & (1 << i):
                            swaps[i, a] = bit_set(words[a], row_place(t, i))
                for c in range(count):
                    xs = {v: buffer[c, v] for v in members}
                    for i in bits:
                        for a in members:
                            if a & (1 << i):
                                continue
                            b = a | (1 << i)
                            x, y = xs[a], xs[b]
                            xs[a] = jnp.where(swaps[i, a], y, x)
                            xs[b] = jnp.where(swaps[i, a], x, y)
                    for v in members:
                        buffer[c, v] = xs[v]
        for v in range(VREGS):
            moved = lane_phase(t, v, lambda c: buffer[c, v])
            if t < 8:
                for c in range(count):
                    buffer[c, v] = moved[c]
            else:
                finish(v, moved)


def plan_kernel(
    packed, offsets,
    near_out, ends_out, frac_out, counts_out,
    index_out, tags,
    moves, chunks,
):
    lane = lane_ids()
    sub = sublane_ids()
    moves[...] = lax.shift_right_logical(packed[...], 29)
    slots = lax.shift_right_logical(packed[...], 16) & (CAP - 1)
    stay = jnp.where(moves[...] == 0, 1.0, 0.0)
    before = jnp.where(
        lax.broadcasted_iota(i32, (128, 128), 0) < lax.broadcasted_iota(i32, (128, 128), 1), 1.0, 0.0
    )
    rank = jnp.dot(stay, before, preferred_element_type=f32)
    above = jnp.where(
        lax.broadcasted_iota(i32, (256, 256), 1) < lax.broadcasted_iota(i32, (256, 256), 0), 1.0, 0.0
    )
    totals = jnp.broadcast_to(jnp.sum(stay, axis=1, keepdims=True), (256, 128))
    rank = rank + jnp.dot(above, totals, preferred_element_type=f32)
    rank = rank.astype(i32)
    counts = []
    for k in range(4):
        count = jnp.sum(jnp.where(moves[...] == k + 1, 1.0, 0.0)).astype(i32)
        counts.append(count)
        counts_out[k] = count
    hole = rank + counts[0]
    filled = counts[0]
    for k in range(1, 4):
        hole = hole + jnp.where(rank >= k * CAP - filled, counts[k], 0)
        filled = filled + counts[k]
    target = jnp.where(moves[...] > 0, (moves[...] - 1) * CAP + slots, hole)
    number = lax.broadcasted_iota(i32, (256, 128), 0) * 128 + lax.broadcasted_iota(i32, (256, 128), 1)
    cell = packed[...] & 65535
    row = (cell.astype(f32) * (1.0 / COLS)).astype(i32)
    row = row - jnp.where(row * COLS > cell, 1, 0)
    row = row + jnp.where((row + 1) * COLS <= cell, 1, 0)
    col = cell - row * COLS
    part = lax.shift_right_logical(col, 7)
    edge = jnp.where(row == 0, 0, 1)
    inner = (row > 0) & (row < ROWS - 1)
    spot = jnp.where(inner, 8 + part * ROWS + row, 2 * part + edge) * 128 + (col & 127)
    keys = []
    for v in range(VREGS):
        part = slice(v * 8, v * 8 + 8)
        keys.append(spot[part].astype(f32))
        tags[v] = lax.shift_left(target[part], 15) | number[part]
        frac_out[0, v] = offsets[0, part]
        frac_out[1, v] = offsets[1, part]
    keys, _, _ = sort_network(keys, (frac_out.at[0], frac_out.at[1], tags), None)
    for v in range(VREGS):
        spots = lax.shift_right_logical(keys[v].astype(i32), 7)
        near_out[v] = spots
        chunks[pl.ds(v, 8, stride=32), :] = lax.shift_right_logical(spots, 7).astype(f32)
    for half in range(2):
        turned = jnp.transpose(chunks[half * 128 : half * 128 + 128, :])
        ends_out[half : half + 1, :] = jnp.min(turned, axis=0, keepdims=True).astype(i32)
        ends_out[half + 2 : half + 3, :] = jnp.max(turned, axis=0, keepdims=True).astype(i32)

    plan_moves(lambda v: lax.shift_right_logical(tags[v], 15), index_out)


def plan_moves(rank, index_out):
    keys = [rank(v).astype(f32) for v in range(VREGS)]

    def record(t, v, index):
        index_out[t, v] = index

    _, words, sub_words = sort_network(keys, (), record)
    for v in range(VREGS):
        index_out[9, v] = words[v]
        index_out[10, v] = sub_words[v]


def plan(cells, offsets, moves, slots):
    packed = cells | lax.shift_left(slots, 16) | lax.shift_left(moves, 29)
    vmem = pl.BlockSpec(memory_space=pltpu.VMEM)
    smem = pl.BlockSpec(memory_space=pltpu.SMEM)
    return pl.pallas_call(
        plan_kernel,
        out_shape=[
            jax.ShapeDtypeStruct((VREGS, 8, 128), i32),
            jax.ShapeDtypeStruct((4, 128), i32),
            jax.ShapeDtypeStruct((2, VREGS, 8, 128), f32),
            jax.ShapeDtypeStruct((4,), i32),
            jax.ShapeDtypeStruct((11, VREGS, 8, 128), i32),
            jax.ShapeDtypeStruct((VREGS, 8, 128), i32),
        ],
        in_specs=[vmem] * 2,
        out_specs=[vmem, vmem, vmem, smem, vmem, vmem],
        scratch_shapes=[pltpu.VMEM((256, 128), i32), pltpu.VMEM((256, 128), f32)],
        compiler_params=pltpu.CompilerParams(vmem_limit_bytes=32 << 20),
        cost_estimate=pl.CostEstimate(flops=20_000_000, bytes_accessed=8_000_000, transcendentals=0),
        name="plan",
    )(packed.reshape(256, 128), offsets.reshape(2, 256, 128))


def pack_kernel(ocean, mass, momentum, out):
    lane = lax.broadcasted_iota(i32, (8, 128), 1)
    tiles = LON * BLOCKS

    def tile(part, k):
        k = k % tiles
        return ocean[part, :, 128 * k : 128 * k + 128]

    spots = (0, 1, 4, 5)
    for b in range(LON):
        rim = jnp.zeros((8, 128), f32)
        for part in range(4):
            for k in range(BLOCKS):
                column = (part * BLOCKS + k) * 128
                out[b, :, column : column + 128] = tile(part, BLOCKS * b + k)
            spot = spots[part]
            rim = jnp.where(lane == spot, pltpu.roll(tile(part, BLOCKS * b - 1), spot + 1, 1), rim)
            rim = jnp.where(lane == spot + 2, pltpu.roll(tile(part, BLOCKS * b + BLOCKS), spot + 2, 1), rim)
        out[b, :, 4 * COLS : 4 * COLS + 128] = rim
    lanes = lax.broadcasted_iota(i32, (ROWS, 128), 1)
    beside = jnp.ones((ROWS, 128), f32)
    for side in range(2):
        column = 0 if side else COLS - 128
        sources = [mass[:, column : column + 128]] * 2 + [
            momentum[part, :, column : column + 128] for part in range(2)
        ]
        for source, spot in zip(sources, spots):
            spot = spot + 2 * side
            shift = spot if side else spot + 1
            beside = jnp.where(lanes == spot, pltpu.roll(source, shift, 1), beside)
    turned = jnp.transpose(beside)[0:8]
    for b in range(LON):
        out[b, :, 4 * COLS + 128 : 4 * COLS + 256] = turned


def pack(ocean, mass, momentum):
    vmem = pl.BlockSpec(memory_space=pltpu.VMEM)
    return pl.pallas_call(
        pack_kernel,
        out_shape=jax.ShapeDtypeStruct((LON, 8, 4 * COLS + 256), f32),
        in_specs=[vmem] * 3,
        out_specs=vmem,
        name="pack",
    )(ocean, mass, momentum)


def drive(momentum, stress, mass, current):
    return (momentum + step_dt * stress + step_dt * drag_coef * mass * current) / (
        mass * (1.0 + step_dt * drag_coef)
    )


def table_kernel(forcing, mass, momentum, table, first_edge, last_edge):
    lane = lax.broadcasted_iota(i32, (ROWS, 128), 1)
    rim = forcing[:, :, 4 * COLS : 4 * COLS + 128].reshape(ROWS, 128)
    here = lax.axis_index("lon")
    west = forcing[lax.rem(here + LON - 1, LON), :, 4 * COLS + 128 : 4 * COLS + 256]
    east = forcing[lax.rem(here + 1, LON), :, 4 * COLS + 128 : 4 * COLS + 256]
    beside = jnp.where((sublane_ids() & 2) == 0, west, east)
    beside = jnp.concatenate([beside] + [jnp.ones((120, 128), f32)], axis=0)
    beside = jnp.transpose(beside)
    rim = drive(pltpu.roll(beside, 124, 1), pltpu.roll(rim, 124, 1), beside, rim)
    for part in range(2):
        blocks, after, before = [], [], []
        for k in range(BLOCKS):
            column = 128 * k
            current = forcing[:, :, COLS * part + column : COLS * part + column + 128]
            stress = forcing[:, :, COLS * (2 + part) + column : COLS * (2 + part) + column + 128]
            block = drive(
                momentum[part, :, column : column + 128],
                stress.reshape(ROWS, 128),
                mass[:, column : column + 128],
                current.reshape(ROWS, 128),
            )
            blocks.append(block)
            after.append(pltpu.roll(block, 1, 1))
            before.append(pltpu.roll(block, 127, 1))
        left = [pltpu.roll(rim, 127, 1) if part else rim] + after[:-1]
        right = before[1:] + [pltpu.roll(rim, 125 - part, 1)]
        for k in range(BLOCKS):
            shifted = (
                jnp.where(lane == 0, left[k], after[k]),
                blocks[k],
                jnp.where(lane == 127, right[k], before[k]),
            )
            for q in range(3):
                plane = part * 3 + q
                for r in range(0, ROWS, 8):
                    table[pl.ds((ROWS * k + r) * 8 + plane, 8, stride=8), :] = shifted[q][r : r + 8]
    for plane in (6, 7):
        for r in range(0, PLANE, 8):
            table[pl.ds(r * 8 + plane, 8, stride=8), :] = jnp.zeros((8, 128), f32)
    for k in range(BLOCKS):
        top, end = ROWS * k * 8, (ROWS * k + ROWS - 1) * 8
        first_edge[8 * k : 8 * k + 8, :] = table[top : top + 8, :]
        last_edge[8 * k : 8 * k + 8, :] = table[end : end + 8, :]


def node_table(forcing, mass, momentum):
    vmem = pl.BlockSpec(memory_space=pltpu.VMEM)
    return pl.pallas_call(
        table_kernel,
        out_shape=[
            jax.ShapeDtypeStruct((8 * PLANE, 128), f32),
            jax.ShapeDtypeStruct((24, 128), f32),
            jax.ShapeDtypeStruct((24, 128), f32),
        ],
        in_specs=[vmem] * 3,
        out_specs=[vmem] * 3,
        compiler_params=pltpu.CompilerParams(vmem_limit_bytes=40 << 20),
        name="table",
    )(forcing, mass, momentum)


def spline(frac):
    lower = 0.5 * (0.5 - frac) * (0.5 - frac)
    middle = 0.75 - frac * frac
    upper = 0.5 * (0.5 + frac) * (0.5 + frac)
    return (lower, middle, upper)


def interpolate_group(g, ends, near, frac, nodes, address, samples, state):
    half = lax.shift_right_logical(g, 4)
    low = (g & 15) * 8
    start = (g & 3) * 64 + lax.shift_right_logical(g, 2)
    first = [ends[half, low + j] for j in range(8)]
    last = [ends[half + 2, low + j] for j in range(8)]
    span = last[0] - first[0]
    for j in range(1, 8):
        span = jnp.maximum(span, last[j] - first[j])

    def trip(step, sums):
        sums = list(sums)
        for j in range(8):
            spot = near[pl.ds(start + 8 * j, 8, stride=0), :]
            lanes = spot & 127
            chunk = lax.shift_right_logical(spot, 7)
            for more in range(3):
                here = jnp.minimum(first[j] + 3 * step + more, last[j])
                base = address(here)
                inside = chunk == here
                for r in range(3):
                    tile = nodes[pl.ds(pl.multiple_of((base + r - 1) * 8, 8), 8), :]
                    sums[3 * j + r] = jnp.where(inside, from_lanes(tile, lanes), sums[3 * j + r])
        return tuple(sums)

    trips = lax.shift_right_logical(span * 171, 9) + 1
    sums = trip(0, tuple(jnp.zeros((8, 128), f32) for _ in range(24)))
    sums = lax.fori_loop(1, trips, trip, sums)
    for j in range(8):
        for r in range(3):
            samples[pl.ds(r * 64 + j, 8, stride=8), :] = sums[3 * j + r]
    rows = pl.ds(start, 8, stride=8)
    d_row = frac[0, rows, :]
    d_col = frac[1, rows, :]
    w_row = spline(d_row)
    w_col = spline(d_col)
    arm_row = [4.0 * w_row[r] * (r - 1 - d_row) for r in range(3)]
    arm_col = [4.0 * w_col[q] * (q - 1 - d_col) for q in range(3)]
    speeds = []
    affines = []
    for part in range(2):
        speed = along_row = along_col = None
        for q in range(3):
            plane = part * 3 + q
            got = [samples[r * 64 + plane * 8 : r * 64 + plane * 8 + 8, :] for r in range(3)]
            plain = w_row[0] * got[0] + w_row[1] * got[1] + w_row[2] * got[2]
            tilted = arm_row[0] * got[0] + arm_row[1] * got[1] + arm_row[2] * got[2]
            terms = (w_col[q] * plain, w_col[q] * tilted, arm_col[q] * plain)
            if q == 0:
                speed, along_row, along_col = terms
            else:
                speed = speed + terms[0]
                along_row = along_row + terms[1]
                along_col = along_col + terms[2]
        speeds.append(speed)
        affines += [along_row, along_col]
    values = [d_row + step_dt * speeds[0], d_col + step_dt * speeds[1]] + speeds + affines
    for c in range(8):
        state[c, rows, :] = values[c]


def group_first(g, ends):
    return ends[lax.shift_right_logical(g, 4), (g & 15) * 8]


def inner_kernel(ends, table, near, frac, state, samples):
    def group(g, carry):
        @pl.when(group_first(g, ends) >= 8)
        def _():
            interpolate_group(
                g, ends, near, frac, table, lambda chunk: chunk - 8, samples, state
            )

        return carry

    lax.fori_loop(0, VREGS, group, 0)


def inner(ends, table, near, frac):
    vmem = pl.BlockSpec(memory_space=pltpu.VMEM)
    smem = pl.BlockSpec(memory_space=pltpu.SMEM)
    return pl.pallas_call(
        inner_kernel,
        out_shape=jax.ShapeDtypeStruct((8, 256, 128), f32),
        in_specs=[smem] + [vmem] * 3,
        out_specs=vmem,
        scratch_shapes=[pltpu.VMEM((192, 128), f32)],
        compiler_params=pltpu.CompilerParams(vmem_limit_bytes=24 << 20),
        cost_estimate=pl.CostEstimate(flops=20_000_000, bytes_accessed=8_000_000, transcendentals=0),
        name="inner",
    )(ends, table, near.reshape(256, 128), frac.reshape(2, 256, 128))


def transfer_kernel(
    ends, counts,
    table, above, below, near, frac, early, index,
    state, north, south, east, west,
    nodes, samples, columns, buffer,
):
    for c in range(8):
        state[c] = early[c]
    nodes[0 : 8 * PLANE, :] = table[...]

    def fill(spot, tile):
        nodes[(PLANE + spot) * 8 : (PLANE + spot) * 8 + 8, :] = tile

    for k in range(BLOCKS):
        top, end = ROWS * k * 8, (ROWS * k + ROWS - 1) * 8
        fill(8 * k, above[8 * k : 8 * k + 8, :])
        fill(8 * k + 1, table[top : top + 8, :])
        fill(8 * k + 2, table[top + 8 : top + 16, :])
        fill(8 * k + 4, table[end - 8 : end, :])
        fill(8 * k + 5, table[end : end + 8, :])
        fill(8 * k + 6, below[8 * k : 8 * k + 8, :])

    def address(chunk):
        return jnp.where(chunk < 8, PLANE + 1 + 4 * chunk, jnp.maximum(chunk - 8, 1))

    def group(g, carry):
        @pl.when(group_first(g, ends) < 8)
        def _():
            interpolate_group(g, ends, near, frac, nodes, address, samples, state)

        return carry

    lax.fori_loop(0, VREGS, group, 0)

    direction = lax.shift_right_logical(sublane_ids(), 1)
    count = jnp.where(
        direction < 2,
        jnp.where(direction == 0, counts[0], counts[1]),
        jnp.where(direction == 2, counts[2], counts[3]),
    )
    slot = (sublane_ids() & 1) * 4096 + lane_ids()

    def finish(v, moved):
        kept = slot + v * 128 < count
        for c in range(8):
            columns[pl.ds(v * 8 + c, 8, stride=256), :] = jnp.where(kept, moved[c], 0.0)

    apply_network(
        8,
        lambda c, v: state[c, 8 * v : 8 * v + 8, :],
        buffer, index, index.at[9], index.at[10], finish,
    )
    for k, out in enumerate((north, south, east, west)):
        for j in range(64):
            base = (k * 64 + j) * 8
            out[:, 128 * j : 128 * j + 128] = columns[base : base + 8, :]


def transfer(ends, counts, table, above, below, near, frac, early, index):
    vmem = pl.BlockSpec(memory_space=pltpu.VMEM)
    smem = pl.BlockSpec(memory_space=pltpu.SMEM)
    return pl.pallas_call(
        transfer_kernel,
        out_shape=[jax.ShapeDtypeStruct((8, 256, 128), f32)]
        + [jax.ShapeDtypeStruct((8, CAP), f32)] * 4,
        in_specs=[smem] * 2 + [vmem] * 7,
        out_specs=[vmem] * 5,
        scratch_shapes=[
            pltpu.VMEM((8 * EDGE_PLANE, 128), f32),
            pltpu.VMEM((192, 128), f32),
            pltpu.VMEM((2048, 128), f32),
            pltpu.VMEM((8, VREGS, 8, 128), f32),
        ],
        compiler_params=pltpu.CompilerParams(vmem_limit_bytes=32 << 20),
        cost_estimate=pl.CostEstimate(flops=10_000_000, bytes_accessed=8_000_000, transcendentals=0),
        name="transfer",
    )(
        ends, counts, table, above, below,
        near.reshape(256, 128), frac.reshape(2, 256, 128), early, index,
    )


def restore_kernel(state, offsets, tags, out, columns, buffer, index):
    plan_moves(lambda v: tags[v] & 32767, index)

    def finish(v, moved):
        for c in range(2):
            frac = offsets[c, pl.ds(v, 8, stride=32), :]
            columns[pl.ds(v * 8 + c, 8, stride=256), :] = frac + step_dt * moved[c]
        for c in range(6):
            columns[pl.ds(v * 8 + c + 2, 8, stride=256), :] = moved[c]

    apply_network(
        6,
        lambda c, v: state[c + 2, 8 * v : 8 * v + 8, :],
        buffer, index, index.at[9], index.at[10], finish,
    )
    for j in range(256):
        out[:, 128 * j : 128 * j + 128] = columns[8 * j : 8 * j + 8, :]


def restore(state, offsets, tags):
    vmem = pl.BlockSpec(memory_space=pltpu.VMEM)
    return pl.pallas_call(
        restore_kernel,
        out_shape=jax.ShapeDtypeStruct((8, 4 * CAP), f32),
        in_specs=[vmem] * 3,
        out_specs=vmem,
        scratch_shapes=[
            pltpu.VMEM((2048, 128), f32),
            pltpu.VMEM((6, VREGS, 8, 128), f32),
            pltpu.VMEM((11, VREGS, 8, 128), i32),
        ],
        compiler_params=pltpu.CompilerParams(vmem_limit_bytes=32 << 20),
        cost_estimate=pl.CostEstimate(flops=10_000_000, bytes_accessed=4_000_000, transcendentals=0),
        name="restore",
    )(state, offsets.reshape(2, 256, 128), tags)


def from_behind(block, axis, distance):
    devices = range(lax.axis_size(axis))
    route = [(i - distance, i) for i in devices if i - distance in devices]
    return lax.ppermute(block, axis, route)


def passed_along(value, axis, by):
    count = lax.axis_size(axis)
    return lax.ppermute(value, axis, [(i, (i + by) % count) for i in range(count)])


def shards(ocean, grid_mass, grid_momentum, cells, offsets, moves, slots):
    outgoing = pack(ocean, grid_mass, grid_momentum)
    forcing = lax.all_to_all(outgoing, "lon", 0, 0)
    near, ends, frac, counts, index, tags = plan(cells, offsets, moves, slots)
    forcing, near = lax.optimization_barrier((forcing, near))
    table, first_edge, last_edge = node_table(forcing, grid_mass, grid_momentum)
    above = from_behind(last_edge, "lat", 1)
    below = from_behind(first_edge, "lat", -1)
    early = inner(ends, table, near, frac)
    state, north, south, east, west = transfer(
        ends, counts, table, above, below, near, frac, early, index
    )
    north = from_behind(north, "lat", 1)
    south = from_behind(south, "lat", -1)
    east = passed_along(east, "lon", 1)
    west = passed_along(west, "lon", -1)
    parcels = restore(state, offsets, tags)
    return (parcels, jnp.concatenate([north, south, east, west], axis=1))


def solution(mesh):
    in_specs = (
        P(None, ("lat", "lon"), None),
        P("lat", "lon"),
        P(None, "lat", "lon"),
        P(("lat", "lon")),
        P(None, ("lat", "lon")),
        P(("lat", "lon")),
        P(("lat", "lon")),
    )
    out_specs = (P(None, ("lat", "lon")), P(None, ("lat", "lon")))
    return jax.shard_map(shards, mesh=mesh, in_specs=in_specs, out_specs=out_specs, check_vma=False)
```
